512 devices in a mesh: dom: 128 (over z, y_lo, x), cls: 4 (over y_hi, core).
Axes of the slice: x: 4, y: 8 (y_hi: 2, y_lo: 4; y = y_hi * 4 + y_lo), z: 8, core: 2. Of those that a mesh axis runs over, the one named last changes fastest.
Arguments:
- images: bfloat16 [65536, 4096], P(('dom', 'cls')), may hold values from -96 to 96
- destinations: int32 [65536, 1], P(('dom', 'cls')), may hold values from 0 to 127; in each aligned block of 128 rows (0 to 127, 128 to 255, ...) at most 2 rows name the same one
- group_ids: int32 [65536], P(('dom', 'cls')), may hold values from 0 to 15
- offsets: int32 [3, 2], replicated, may hold values from -4 to 4
- inv_noise: float32 [2048], replicated, may hold values from 0.02 to 0.2
- ctf_table: float32 [16, 2048], replicated, may hold values from -1 to 1
- references: bfloat16 [288, 4096], P('cls', 'dom'), may hold values from -16 to 16
Outputs:
- posteriors: float32 [131072, 288], P('dom', 'cls')
- log_norms: float32 [131072], P('dom')
The draws below stay inside these ranges and needn't reach their ends.
Inputs may be any that keep to these rules, and one draw needn't show every extreme that they name: `destinations`: in the rows of one device no destination is named more than 2 times.
All inputs are finite; a program needn't handle non-finite values.
Results may differ from the reference program's by a relative error of at most 0.00061.
Values may be sent and summed in bfloat16 or wider, within the bound.
No kernel may reach another device: no remote copies, remote signals or barrier semaphores. Data moves between devices by JAX's collectives and lax.ppermute only.
A program may use at most 64 MiB of HBM per device.

```python
import math
import jax
import jax.numpy as jnp
import numpy as np
from jax import lax

SIDE = 64
F = 2048
ROT = 36
NT = 3
G = 16
P_DEV = 128
CAP = 2
SLOTS = 256
K = 8
PARTICLES = 65536
ROWS_OUT = 131072
N_DOM = 128
N_CLS = 4


def class_amplitudes(key):
    first_key = jax.random.fold_in(jax.random.fold_in(key, 201), 0)
    amplitudes = jnp.exp(jax.random.uniform(first_key, (K,), jnp.float32, math.log(0.2), math.log(0.55)))
    return amplitudes


def reference_rows(key):
    amplitudes = class_amplitudes(key)
    first_key = jax.random.fold_in(jax.random.fold_in(key, 202), 0)
    base = jnp.clip(jax.random.normal(first_key, (K * ROT, 2 * F), jnp.float32), -6.0, 6.0)
    row_amplitude = jnp.repeat(amplitudes, ROT)
    return base * row_amplitude[:, None]


def ctf_values(key):
    return jax.random.uniform(jax.random.fold_in(key, 203), (G, F), jnp.float32, -1.0, 1.0)


def group_values(key):
    return jax.random.randint(jax.random.fold_in(key, 204), (PARTICLES,), 0, G).astype(jnp.int32)


def offset_values(key):
    return jax.random.randint(jax.random.fold_in(key, 205), (NT, 2), -4, 5).astype(jnp.int32)


def phase_values(offsets):
    freq_index = jnp.arange(F, dtype=jnp.int32)
    half_side = SIDE // 2
    row_freq = freq_index // half_side
    col_freq = freq_index % half_side
    row_freq = jnp.where(row_freq >= half_side, row_freq - SIDE, row_freq)
    turns = jnp.mod(offsets[:, 0:1] * row_freq[None, :] + offsets[:, 1:2] * col_freq[None, :], SIDE)
    angles = turns.astype(jnp.float32) * (2.0 * math.pi / SIDE)
    return (jnp.cos(angles), jnp.sin(angles))


def draw_references(key, part):
    return reference_rows(key).astype(jnp.bfloat16)


def draw_ctf_table(key, part):
    return ctf_values(key)


def draw_group_ids(key, part):
    return group_values(key)


def draw_offsets(key, part):
    return offset_values(key)


def draw_images(key, part):
    refs = reference_rows(key).astype(jnp.bfloat16).astype(jnp.float32)
    ctf = ctf_values(key)
    groups = group_values(key)
    cosines, sines = phase_values(offset_values(key))
    match_key, shift_key, noise_key = jax.random.split(jax.random.fold_in(key, 206), 3)
    matched = jax.random.randint(match_key, (PARTICLES,), 0, K * ROT).astype(jnp.int32)
    shift_pick = jax.random.randint(shift_key, (PARTICLES,), 0, NT).astype(jnp.int32)
    block_rows = 512

    def one_block(block_index):
        start = (block_index * block_rows).astype(jnp.int32)
        match_rows = lax.dynamic_slice_in_dim(matched, start, block_rows, 0)
        group_rows = lax.dynamic_slice_in_dim(groups, start, block_rows, 0)
        shift_rows = lax.dynamic_slice_in_dim(shift_pick, start, block_rows, 0)
        chosen = refs[match_rows]
        ref_real = chosen[:, :F]
        ref_imag = chosen[:, F:]
        ctf_rows = ctf[group_rows]
        cosine = cosines[shift_rows]
        sine = sines[shift_rows]
        signal_real = ctf_rows * (ref_real * cosine + ref_imag * sine)
        signal_imag = ctf_rows * (ref_imag * cosine - ref_real * sine)
        block_key = jax.random.fold_in(noise_key, block_index)
        noise = jnp.clip(jax.random.normal(block_key, (block_rows, 2 * F), jnp.float32), -6.0, 6.0)
        return jnp.concatenate([signal_real, signal_imag], axis=1) + noise
    values = lax.map(one_block, jnp.arange(PARTICLES // block_rows, dtype=jnp.int32))
    return values.reshape(PARTICLES, 2 * F).astype(jnp.bfloat16)


def deal_out(key, own, number, rows, count, top, most, slope):
    ranking = jax.random.permutation(key, count)
    heavy_load, ordinary = load_shares(count, rows * top, most, slope, True), load_shares(count, rows * top, most, slope, False)
    places = jnp.arange(count)

    def named(tallies, offset_by):
        used = int((tallies > 0).sum())
        fixed = max(1, used // 4)
        moved = fixed + (places - fixed + offset_by * (used - fixed)) % max(1, count - fixed)
        return jnp.zeros((count,), jnp.int32).at[ranking[jnp.where(places < fixed, places, moved)]].set(jnp.asarray(tallies, jnp.int32))

    tallies = jnp.where(number % 4 == 0, named(heavy_load, number // 4), named(ordinary, number - number // 4 - 1))
    mixed = jax.random.permutation(jax.random.fold_in(own, 3), count)
    giver, receiver = mixed[0:count // 2 * 2:2], mixed[1:count // 2 * 2:2]
    room = jnp.minimum(tallies[giver] - 1, most - tallies[receiver]) // 2
    room = jnp.where((giver == ranking[0]) | (receiver == ranking[0]) | (tallies[receiver] == 0), 0, jnp.maximum(room, 0))
    moved = jax.random.randint(jax.random.fold_in(own, 4), (count // 2,), 0, 1 << 20) % (room + 1)
    tallies = tallies.at[giver].add(-moved).at[receiver].add(moved)
    labels = jnp.searchsorted(jnp.cumsum(tallies), jnp.arange(rows * top), side="right").astype(jnp.int32)
    grid = labels.reshape(top, rows).T
    grid = grid[jax.random.permutation(jax.random.fold_in(own, 1), rows)]
    offset_by = jax.random.randint(jax.random.fold_in(own, 2), (rows, 1), 0, top)
    return jnp.take_along_axis(grid, (jnp.arange(top)[None, :] + offset_by) % top, axis=1)


def load_shares(amount, total, reach, slope, full):
    portions = [(1 << 20) // math.isqrt(standing ** slope) + 1 for standing in range(1, amount + 1)]
    largest = reach if full else min(reach, max(-(-total // amount), total * portions[0] // sum(portions)))
    least = 1 if total - largest >= amount - 1 else 0
    given, spare = [largest] + [least] * (amount - 1), total - largest - least * (amount - 1)
    while spare > 0:
        candidates = [i for i in range(1, amount) if given[i] < largest] or [i for i in range(1, amount) if given[i] < reach]
        whole, budget = sum([portions[i] for i in candidates]), spare
        for i in candidates:
            more = min(reach - given[i], max(1, budget * portions[i] // whole), spare)
            given[i] = given[i] + more
            spare = spare - more
    return np.array(given)


def setup_inputs(seed: int = 0) -> dict:
    key_list = jax.random.split(jax.random.key(seed), 8)
    images = draw_images(jax.random.fold_in(key_list[7], 71), 0)
    destinations_keys = jax.random.split(jax.random.fold_in(key_list[1], 1), PARTICLES // P_DEV)
    destinations_turns = jax.random.permutation(jax.random.fold_in(key_list[1], 3), PARTICLES // P_DEV)
    destinations = jax.vmap(lambda own, number: deal_out(jax.random.fold_in(key_list[1], 2), own, number, P_DEV, N_DOM, 1, CAP, 1))(destinations_keys, destinations_turns).reshape((PARTICLES, 1))
    group_ids = draw_group_ids(jax.random.fold_in(key_list[7], 71), 0)
    offsets = draw_offsets(jax.random.fold_in(key_list[7], 71), 0)
    inv_noise = jnp.clip(jnp.exp(jax.random.uniform(key_list[4], (F,), jnp.float32, math.log(0.02), math.log(0.2))), 0.02, 0.2)
    ctf_table = draw_ctf_table(jax.random.fold_in(key_list[7], 71), 0)
    references = draw_references(jax.random.fold_in(key_list[7], 71), 0)
    return {"images": images, "destinations": destinations, "group_ids": group_ids, "offsets": offsets, "inv_noise": inv_noise, "ctf_table": ctf_table, "references": references}


def phase_tables(offsets):
    freq_index = jnp.arange(F, dtype=jnp.int32)
    half_side = SIDE // 2
    row_freq = freq_index // half_side
    col_freq = freq_index % half_side
    row_freq = jnp.where(row_freq >= half_side, row_freq - SIDE, row_freq)
    turns = jnp.mod(offsets[:, 0:1] * row_freq[None, :] + offsets[:, 1:2] * col_freq[None, :], SIDE)
    angles = turns.astype(jnp.float32) * (2.0 * math.pi / SIDE)
    return jnp.cos(angles), jnp.sin(angles)


def shifted_rows(block_images, weight, cosines, sines):
    real_part = block_images[:, :F].astype(jnp.float32)
    imag_part = block_images[:, F:].astype(jnp.float32)
    pieces = []
    for shift_index in range(NT):
        cosine = cosines[shift_index][None, :]
        sine = sines[shift_index][None, :]
        both = jnp.concatenate([weight * (real_part * cosine - imag_part * sine), weight * (real_part * sine + imag_part * cosine)], axis=1)
        pieces.append(both.astype(jnp.bfloat16))
    return jnp.concatenate(pieces, axis=0)


def reference(images, destinations, group_ids, offsets, inv_noise, ctf_table, references):
    blocks = N_DOM * N_CLS
    target = destinations[:, 0].reshape(blocks, P_DEV)
    target_hot = (target[:, :, None] == jnp.arange(N_DOM, dtype=jnp.int32)[None, None, :]).astype(jnp.int32)
    earlier = jnp.cumsum(target_hot, axis=1) - target_hot
    position_rank = jnp.sum(earlier * target_hot, axis=2)
    block_ids = jnp.arange(blocks, dtype=jnp.int32)
    source_dom = block_ids // N_CLS
    source_cls = block_ids % N_CLS
    out_rows = (target * (N_CLS * SLOTS) + source_cls[:, None] * SLOTS + source_dom[:, None] * CAP + position_rank).reshape(-1).astype(jnp.int32)
    cosines, sines = phase_tables(offsets)
    refs_float = references.astype(jnp.float32)
    squared = refs_float * refs_float
    noise_ctf = inv_noise[None, :] * ctf_table * ctf_table
    doubled = jnp.concatenate([noise_ctf, noise_ctf], axis=1)
    group_norms = jnp.dot(doubled, squared.T, precision=lax.Precision.HIGHEST, preferred_element_type=jnp.float32)
    refs_columns = references.T
    block_rows = 512

    def score_block(inputs):
        block_images, block_groups = inputs
        weight = inv_noise[None, :] * ctf_table[block_groups]
        shifted = shifted_rows(block_images, weight, cosines, sines)
        cross = jnp.dot(shifted, refs_columns, preferred_element_type=jnp.float32).reshape(NT, block_rows, K * ROT)
        scores = cross - 0.5 * group_norms[block_groups][None, :, :]
        row_peak = jnp.max(scores, axis=(0, 2))
        row_total = jnp.sum(jnp.exp(scores - row_peak[None, :, None]), axis=(0, 2))
        log_norm = row_peak + jnp.log(row_total)
        posterior = jnp.sum(jnp.exp(scores - log_norm[None, :, None]), axis=0)
        return posterior, log_norm

    posterior_all, norm_all = lax.map(score_block, (images.reshape(-1, block_rows, 2 * F), group_ids.reshape(-1, block_rows)))
    posteriors = jnp.zeros((ROWS_OUT, K * ROT), jnp.float32).at[out_rows].set(posterior_all.reshape(-1, K * ROT))
    log_norms = jnp.zeros((ROWS_OUT,), jnp.float32).at[out_rows].set(norm_all.reshape(-1))
    return posteriors, log_norms
```

```python
import math

import jax
import jax.numpy as jnp
from jax import lax
from jax.experimental import pallas as pl
from jax.experimental.pallas import tpu as pltpu
from jax.sharding import Mesh
from jax.sharding import PartitionSpec as P

SIDE = 64
F = 2048
NT = 3
G = 16
COLS = 2 * F
PART = 128
JBLK = 72
SUB = 18
PADJ = 32
NGRP = 16
WIDE = NGRP * PADJ
SENT = 4 * (JBLK + 1)
SPLIT_AXES = ("z", "yl", "x", "yh", "core")
DOM = ("z", "yl", "x")
CLS = ("yh", "core")
HIGH = lax.Precision.HIGHEST
NT_DIMS = (((1,), (1,)), ((), ()))


def phase_tables(offsets):
    freq_index = jnp.arange(F, dtype=jnp.int32)
    half_side = SIDE // 2
    row_freq = freq_index // half_side
    col_freq = freq_index % half_side
    row_freq = jnp.where(row_freq >= half_side, row_freq - SIDE, row_freq)
    turns = jnp.mod(offsets[:, 0:1] * row_freq[None, :] + offsets[:, 1:2] * col_freq[None, :], SIDE)
    angles = turns.astype(jnp.float32) * (2.0 * math.pi / SIDE)
    return (jnp.cos(angles), jnp.sin(angles))


def shift_kernel(images_ref, hot_ref, noise_ref, ctf_ref, cos_ref, sin_ref, out_ref):
    step = 256

    def body(n, carry):
        at = pl.multiple_of(n * step, step)
        cols = pl.ds(at, step)
        imag_cols = pl.ds(pl.multiple_of(F + at, step), step)
        ctf_rows = jnp.dot(
            hot_ref[...], ctf_ref[:, cols], precision=HIGH, preferred_element_type=jnp.float32
        )
        weight = noise_ref[:, cols] * ctf_rows
        real_part = images_ref[:, cols].astype(jnp.float32)
        imag_part = images_ref[:, imag_cols].astype(jnp.float32)
        for t in range(NT):
            cosine = cos_ref[t : t + 1, cols]
            sine = sin_ref[t : t + 1, cols]
            rows = pl.ds(t * PART, PART)
            out_ref[rows, cols] = (weight * (real_part * cosine - imag_part * sine)).astype(
                jnp.bfloat16
            )
            out_ref[rows, imag_cols] = (weight * (real_part * sine + imag_part * cosine)).astype(
                jnp.bfloat16
            )
        return carry

    lax.fori_loop(0, F // step, body, 0)


def score_kernel(
    shifted_ref, mine_ref, other_ref, noise_ref, hot_ref, chosen_ref, perm_ref, out_ref, refs, acc, norm
):
    def place(zy, carry):
        cols = pl.ds(pl.multiple_of(zy * 128, 128), 128)
        for src, from_ref in enumerate((mine_ref, other_ref)):
            for x in range(4):
                for yh in range(2):
                    group = (src * 4 + x) * 2 + yh
                    refs[pl.ds(group * PADJ, SUB), cols] = from_ref[x, zy * 2 + yh]
        return carry

    lax.fori_loop(0, 32, place, 0)
    acc[...] = jnp.zeros_like(acc)
    norm[...] = jnp.zeros_like(norm)
    step = 512

    def body(n, carry):
        at = pl.multiple_of(n * step, step)
        cols = pl.ds(at, step)
        piece = refs[:, cols]
        acc[...] += lax.dot_general(
            shifted_ref[:, cols], piece, NT_DIMS, preferred_element_type=jnp.float32
        )
        wide = piece.astype(jnp.float32)
        square = wide * wide
        high = square.astype(jnp.bfloat16)
        low = (square - high.astype(jnp.float32)).astype(jnp.bfloat16)
        terms = noise_ref[:, cols]
        first = terms.astype(jnp.bfloat16)
        rest = terms - first.astype(jnp.float32)
        second = rest.astype(jnp.bfloat16)
        third = (rest - second.astype(jnp.float32)).astype(jnp.bfloat16)
        parts = jnp.concatenate([first, second, third], axis=0)
        norm[...] += lax.dot_general(
            parts, high, NT_DIMS, preferred_element_type=jnp.float32
        ) + lax.dot_general(parts, low, NT_DIMS, preferred_element_type=jnp.float32)
        return carry

    lax.fori_loop(0, COLS // step, body, 0)
    norms = norm[0:G, :] + (norm[G : 2 * G, :] + norm[2 * G : 3 * G, :])
    lane = lax.broadcasted_iota(jnp.int32, (PART, WIDE), 1)
    real = (lane & (PADJ - 1)) < SUB
    selected = 0.5 * jnp.dot(hot_ref[...], norms, precision=HIGH, preferred_element_type=jnp.float32)
    scores = [
        jnp.where(real, acc[pl.ds(t * PART, PART), :] - selected, -jnp.inf) for t in range(NT)
    ]
    peak = jnp.max(
        jnp.maximum(jnp.maximum(scores[0], scores[1]), scores[2]), axis=1, keepdims=True
    )
    raised = sum(jnp.exp(s - peak) for s in scores)
    log_norm = peak + jnp.log(jnp.sum(raised, axis=1, keepdims=True))
    posterior = sum(jnp.exp(s - log_norm) for s in scores)
    posterior = jnp.where(lane == SUB, log_norm, posterior)
    slots = jnp.dot(chosen_ref[...], posterior, precision=HIGH, preferred_element_type=jnp.float32)
    out_ref[...] = jnp.dot(slots, perm_ref[...], precision=HIGH, preferred_element_type=jnp.float32)


def slot_choice(destinations):
    target = destinations[:, 0]
    same = target[:, None] == target[None, :]
    local_index = jnp.arange(PART, dtype=jnp.int32)
    lower = local_index[:, None] > local_index[None, :]
    rank = jnp.sum(jnp.where(same & lower, 1, 0), axis=1)
    slot_of = target * 2 + rank
    return (jnp.arange(2 * PART, dtype=jnp.int32)[:, None] == slot_of[None, :]).astype(jnp.float32)


def column_order():
    core = lax.axis_index("core")
    column = jnp.arange(SENT, dtype=jnp.int32)
    block = column // (JBLK + 1)
    within = column % (JBLK + 1)
    source = jnp.where(block % 2 == core, 0, 1)
    group = (source * 4 + within // SUB) * 2 + block // 2
    lane = jnp.where(within == JBLK, SUB, group * PADJ + within % SUB)
    return (jnp.arange(WIDE, dtype=jnp.int32)[:, None] == lane[None, :]).astype(jnp.float32)


def shards(images, destinations, group_ids, offsets, inv_noise, ctf_table, references):
    pieces = references.reshape(4, SUB, 32)
    pieces = lax.all_to_all(pieces, "x", split_axis=0, concat_axis=0, tiled=True)
    piece = pieces.transpose(1, 0, 2).reshape(SUB, 128)
    plane = lax.all_to_all(
        jnp.broadcast_to(piece[None], (64, SUB, 128)), ("z", "yl", "yh"), 0, 0, tiled=True
    )
    mine = lax.all_to_all(
        jnp.broadcast_to(plane[None], (4, 64, SUB, 128)), "x", 0, 0, tiled=True
    )
    other = lax.ppermute(mine, "core", [(0, 1), (1, 0)])

    cosines, sines = phase_tables(offsets)
    group_hot = (group_ids[:, None] == jnp.arange(G, dtype=jnp.int32)[None, :]).astype(jnp.float32)
    shifted = pl.pallas_call(
        shift_kernel,
        out_shape=jax.ShapeDtypeStruct((NT * PART, COLS), jnp.bfloat16),
        name="shift",
    )(images, group_hot, inv_noise[None, :], ctf_table, cosines, sines)
    noise_ctf = inv_noise[None, :] * ctf_table * ctf_table
    noise_terms = jnp.concatenate([noise_ctf, noise_ctf], axis=1)
    sends = pl.pallas_call(
        score_kernel,
        out_shape=jax.ShapeDtypeStruct((2 * PART, SENT), jnp.float32),
        scratch_shapes=[
            pltpu.VMEM((WIDE, COLS), jnp.bfloat16),
            pltpu.VMEM((NT * PART, WIDE), jnp.float32),
            pltpu.VMEM((3 * G, WIDE), jnp.float32),
        ],
        name="score",
    )(
        shifted,
        mine,
        other,
        noise_terms,
        group_hot,
        slot_choice(destinations),
        column_order(),
    )
    slots = lax.all_to_all(sends.reshape(PART, 2, SENT), DOM, 0, 0, tiled=True)
    whole = lax.all_to_all(
        slots.reshape(2 * PART, SENT), CLS, split_axis=1, concat_axis=0, tiled=True
    )
    return (whole[:, :JBLK], whole[:, JBLK])


def solution(mesh):
    split = Mesh(mesh.devices.reshape(8, 4, 4, 2, 2), SPLIT_AXES)
    return jax.shard_map(
        shards,
        mesh=split,
        in_specs=(
            P(SPLIT_AXES, None),
            P(SPLIT_AXES, None),
            P(SPLIT_AXES),
            P(),
            P(),
            P(),
            P(CLS, DOM),
        ),
        out_specs=(P(DOM, CLS), P(DOM)),
        check_vma=False,
    )
```

```python
import math

import jax
import jax.numpy as jnp
from jax import lax
from jax.experimental import pallas as pl
from jax.experimental.pallas import tpu as pltpu
from jax.sharding import Mesh
from jax.sharding import PartitionSpec as P

SIDE = 64
F = 2048
NT = 3
G = 16
COLS = 2 * F
PART = 128
JBLK = 72
SUB = 18
ROWS = 40
XCOLS = COLS + 128
PADJ = 48
WIDE = 8 * PADJ
SPLIT_AXES = ("z", "yl", "x", "yh", "core")
DOM = ("z", "yl", "x")
CLS = ("yh", "core")
HIGH = lax.Precision.HIGHEST
NT_DIMS = (((1,), (1,)), ((), ()))


def phase_tables(offsets):
    freq_index = jnp.arange(F, dtype=jnp.int32)
    half_side = SIDE // 2
    row_freq = freq_index // half_side
    col_freq = freq_index % half_side
    row_freq = jnp.where(row_freq >= half_side, row_freq - SIDE, row_freq)
    turns = jnp.mod(offsets[:, 0:1] * row_freq[None, :] + offsets[:, 1:2] * col_freq[None, :], SIDE)
    angles = turns.astype(jnp.float32) * (2.0 * math.pi / SIDE)
    return (jnp.cos(angles), jnp.sin(angles))


def shift_kernel(images_ref, hot_ref, minus_ref, noise_ref, ctf_ref, cos_ref, sin_ref, out_ref):
    step = 256

    def body(n, carry):
        at = pl.multiple_of(n * step, step)
        cols = pl.ds(at, step)
        imag_cols = pl.ds(pl.multiple_of(F + at, step), step)
        ctf_rows = jnp.dot(
            hot_ref[...], ctf_ref[:, cols], precision=HIGH, preferred_element_type=jnp.float32
        )
        weight = noise_ref[:, cols] * ctf_rows
        real_part = images_ref[:, cols].astype(jnp.float32)
        imag_part = images_ref[:, imag_cols].astype(jnp.float32)
        for t in range(NT):
            cosine = cos_ref[t : t + 1, cols]
            sine = sin_ref[t : t + 1, cols]
            rows = pl.ds(t * PART, PART)
            out_ref[rows, cols] = (weight * (real_part * cosine - imag_part * sine)).astype(
                jnp.bfloat16
            )
            out_ref[rows, imag_cols] = (weight * (real_part * sine + imag_part * cosine)).astype(
                jnp.bfloat16
            )
        return carry

    lax.fori_loop(0, F // step, body, 0)
    for t in range(NT):
        out_ref[pl.ds(t * PART, PART), pl.ds(COLS, 128)] = minus_ref[...].astype(jnp.bfloat16)


def layout_kernel(plane_ref, noise_ref, out_ref, rows_ref, small_ref):
    rows_ref[...] = jnp.zeros_like(rows_ref)
    small_ref[...] = jnp.zeros_like(small_ref)
    for zy in range(32):
        for yh in range(2):
            rows_ref[yh * 20 : yh * 20 + SUB, zy * 128 : zy * 128 + 128] = plane_ref[
                zy * 2 + yh
            ].astype(jnp.float32)
    rows = rows_ref[...]
    out_ref[:, :COLS] = rows.astype(jnp.bfloat16)
    square = rows * rows
    high = square.astype(jnp.bfloat16)
    low = (square - high.astype(jnp.float32)).astype(jnp.bfloat16)
    first, second, third = three_parts(noise_ref[...])
    parts = jnp.concatenate(
        [first.astype(jnp.bfloat16), second.astype(jnp.bfloat16), third.astype(jnp.bfloat16)], axis=0
    )
    sums = lax.dot_general(
        parts, high, NT_DIMS, preferred_element_type=jnp.float32
    ) + lax.dot_general(parts, low, NT_DIMS, preferred_element_type=jnp.float32)
    norms = sums[0:G] + (sums[G : 2 * G] + sums[2 * G : 3 * G])
    for k, value in enumerate(three_parts(norms)):
        small_ref[k * G : (k + 1) * G, 0:ROWS] = value
    turned = small_ref[...].T
    out_ref[:, COLS:] = turned[0:ROWS].astype(jnp.bfloat16)


def three_parts(value):
    first = value.astype(jnp.bfloat16).astype(jnp.float32)
    rest = value - first
    second = rest.astype(jnp.bfloat16).astype(jnp.float32)
    return (first, second, rest - second)


def score_kernel(shifted_ref, mine_ref, other_ref, real_ref, chosen_ref, perm_ref, out_ref, refs, acc):
    for src, from_ref in enumerate((mine_ref, other_ref)):
        for x in range(4):
            at = (src * 4 + x) * PADJ
            refs[at : at + ROWS, :] = from_ref[x]
    acc[...] = jnp.zeros_like(acc)
    step = 384

    def body(n, carry):
        cols = pl.ds(pl.multiple_of(n * step, step), step)
        acc[...] += lax.dot_general(
            shifted_ref[:, cols], refs[:, cols], NT_DIMS, preferred_element_type=jnp.float32
        )
        return carry

    lax.fori_loop(0, XCOLS // step, body, 0)
    real = real_ref[...] > 0.0
    scores = [jnp.where(real, acc[t * PART : (t + 1) * PART, :], -jnp.inf) for t in range(NT)]
    peak = jnp.max(
        jnp.maximum(jnp.maximum(scores[0], scores[1]), scores[2]), axis=1, keepdims=True
    )
    raised = sum(jnp.exp(s - peak) for s in scores)
    log_norm = peak + jnp.log(jnp.sum(raised, axis=1, keepdims=True))
    posterior = sum(jnp.exp(s - log_norm) for s in scores)
    lane = lax.broadcasted_iota(jnp.int32, (PART, WIDE), 1)
    posterior = jnp.where(lane == SUB, log_norm, posterior)
    ordered = jnp.dot(posterior, perm_ref[...], precision=HIGH, preferred_element_type=jnp.float32)
    for rank in range(2):
        slots = jnp.dot(
            chosen_ref[rank], ordered, precision=HIGH, preferred_element_type=jnp.float32
        )
        for block in range(4):
            out_ref[block * PART : (block + 1) * PART, rank, :] = slots[
                :, block * 128 : (block + 1) * 128
            ]


def slot_choice(destinations):
    target = destinations[:, 0]
    same = target[:, None] == target[None, :]
    local_index = jnp.arange(PART, dtype=jnp.int32)
    lower = local_index[:, None] > local_index[None, :]
    rank = jnp.sum(jnp.where(same & lower, 1, 0), axis=1)
    slot = jnp.arange(PART, dtype=jnp.int32)[None, :, None]
    ranks = jnp.arange(2, dtype=jnp.int32)[:, None, None]
    chosen = (slot == target[None, None, :]) & (ranks == rank[None, None, :])
    return chosen.astype(jnp.float32)


def column_order():
    core = lax.axis_index("core")
    column = jnp.arange(4 * 128, dtype=jnp.int32)
    block = column // 128
    within = column % 128
    source = jnp.where(block % 2 == core, 0, 1)
    lane = (source * 4 + within // SUB) * PADJ + (block // 2) * 20 + within % SUB
    lane = jnp.where(within == JBLK, SUB, jnp.where(within < JBLK, lane, -1))
    return (jnp.arange(WIDE, dtype=jnp.int32)[:, None] == lane[None, :]).astype(jnp.float32)


def real_lanes():
    within = jnp.arange(WIDE, dtype=jnp.int32) % PADJ
    return ((within < ROWS) & (within % 20 < SUB)).astype(jnp.float32)[None, :]


def shards(images, destinations, group_ids, offsets, inv_noise, ctf_table, references):
    pieces = references.reshape(4, SUB, 32)
    pieces = lax.all_to_all(pieces, "x", split_axis=0, concat_axis=0, tiled=True)
    piece = pieces.transpose(1, 0, 2).reshape(SUB, 128)
    plane = lax.all_to_all(
        jnp.broadcast_to(piece[None], (64, SUB, 128)), ("z", "yl", "yh"), 0, 0, tiled=True
    )

    cosines, sines = phase_tables(offsets)
    group_hot = (group_ids[:, None] == jnp.arange(G, dtype=jnp.int32)[None, :]).astype(jnp.float32)
    lane = jnp.arange(128, dtype=jnp.int32)[None, :]
    minus = jnp.where((lane < 3 * G) & (lane % G == group_ids[:, None]), -0.5, 0.0)
    shifted = pl.pallas_call(
        shift_kernel,
        out_shape=jax.ShapeDtypeStruct((NT * PART, XCOLS), jnp.bfloat16),
        name="shift",
    )(images, group_hot, minus, inv_noise[None, :], ctf_table, cosines, sines)
    noise_ctf = inv_noise[None, :] * ctf_table * ctf_table
    noise_terms = jnp.concatenate([noise_ctf, noise_ctf], axis=1)
    chosen = slot_choice(destinations)
    order = column_order()
    plane, noise_terms, shifted, chosen, order = lax.optimization_barrier(
        (plane, noise_terms, shifted, chosen, order)
    )
    block = pl.pallas_call(
        layout_kernel,
        out_shape=jax.ShapeDtypeStruct((ROWS, XCOLS), jnp.bfloat16),
        scratch_shapes=[
            pltpu.VMEM((ROWS, COLS), jnp.float32),
            pltpu.VMEM((128, 128), jnp.float32),
        ],
        name="layout",
    )(plane, noise_terms)
    mine = lax.all_to_all(jnp.broadcast_to(block[None], (4, ROWS, XCOLS)), "x", 0, 0, tiled=True)
    other = lax.ppermute(mine, "core", [(0, 1), (1, 0)])
    sends = pl.pallas_call(
        score_kernel,
        out_shape=jax.ShapeDtypeStruct((4 * PART, 2, 128), jnp.float32),
        scratch_shapes=[
            pltpu.VMEM((WIDE, XCOLS), jnp.bfloat16),
            pltpu.VMEM((NT * PART, WIDE), jnp.float32),
        ],
        name="score",
    )(shifted, mine, other, real_lanes(), chosen, order)
    whole = lax.all_to_all(sends, CLS + DOM, 0, 0, tiled=True).reshape(8 * PART, 128)
    return (whole[:, :JBLK], whole[:, JBLK])


def solution(mesh):
    split = Mesh(mesh.devices.reshape(8, 4, 4, 2, 2), SPLIT_AXES)
    return jax.shard_map(
        shards,
        mesh=split,
        in_specs=(
            P(SPLIT_AXES, None),
            P(SPLIT_AXES, None),
            P(SPLIT_AXES),
            P(),
            P(),
            P(),
            P(CLS, DOM),
        ),
        out_specs=(P(DOM, CLS), P(DOM)),
        check_vma=False,
    )
```

```python
import math

import jax
import jax.numpy as jnp
from jax import lax
from jax.experimental import pallas as pl
from jax.experimental.pallas import tpu as pltpu
from jax.sharding import Mesh
from jax.sharding import PartitionSpec as P

SIDE = 64
F = 2048
NT = 3
G = 16
PART = 128
JBLK = 72
SUB = 18
ROWS = 2 * JBLK
XF = F // 4
KX = 2 * XF + 128
SPLIT_AXES = ("z", "yl", "x", "yh", "core")
DOM = ("z", "yl", "x")
CLS = ("yh", "core")
HIGH = lax.Precision.HIGHEST
NT_DIMS = (((1,), (1,)), ((), ()))


def by_x(values):
    split = values.reshape(values.shape[:-1] + (16, 4, 32))
    return jnp.moveaxis(split, -2, -3).reshape(values.shape)


def phase_tables(offsets):
    place = jnp.arange(F, dtype=jnp.int32)
    freq_index = (place % XF) // 32 * 128 + place // XF * 32 + place % 32
    half_side = SIDE // 2
    row_freq = freq_index // half_side
    col_freq = freq_index % half_side
    row_freq = jnp.where(row_freq >= half_side, row_freq - SIDE, row_freq)
    turns = jnp.mod(offsets[:, 0:1] * row_freq[None, :] + offsets[:, 1:2] * col_freq[None, :], SIDE)
    angles = turns.astype(jnp.float32) * (2.0 * math.pi / SIDE)
    return (jnp.cos(angles), jnp.sin(angles))


def three_parts(value):
    first = value.astype(jnp.bfloat16).astype(jnp.float32)
    rest = value - first
    second = rest.astype(jnp.bfloat16).astype(jnp.float32)
    return (first, second, rest - second)


def turned(tiles, x):
    return jnp.concatenate([tile[:, x * 32 : x * 32 + 32] for tile in tiles], axis=1)


def shift_kernel(images_ref, hot_ref, minus_ref, noise_ref, ctf_ref, cos_ref, sin_ref, out_ref):
    for quad in range(4):
        real_tiles, imag_tiles = (
            [
                images_ref[:, start + n * 128 : start + n * 128 + 128].astype(jnp.float32)
                for n in range(4)
            ]
            for start in (quad * 512, F + quad * 512)
        )
        for x in range(4):
            cols = slice(x * XF + quad * 128, x * XF + quad * 128 + 128)
            real_part = turned(real_tiles, x)
            imag_part = turned(imag_tiles, x)
            ctf_rows = jnp.dot(
                hot_ref[...], ctf_ref[:, cols], precision=HIGH, preferred_element_type=jnp.float32
            )
            weight = noise_ref[:, cols] * ctf_rows
            at = x * KX + quad * 128
            for t in range(NT):
                cosine = cos_ref[t : t + 1, cols]
                sine = sin_ref[t : t + 1, cols]
                rows = slice(t * PART, (t + 1) * PART)
                out_ref[rows, at : at + 128] = (
                    weight * (real_part * cosine - imag_part * sine)
                ).astype(jnp.bfloat16)
                out_ref[rows, at + XF : at + XF + 128] = (
                    weight * (real_part * sine + imag_part * cosine)
                ).astype(jnp.bfloat16)
    for x in range(4):
        for t in range(NT):
            out_ref[t * PART : (t + 1) * PART, x * KX + 2 * XF : (x + 1) * KX] = minus_ref[
                ...
            ].astype(jnp.bfloat16)


def layout_kernel(plane_ref, noise_ref, out_ref, rows_ref, small_ref):
    for yh in range(2):
        for quad in range(8):
            tiles = [
                plane_ref[(quad * 4 + n) * 2 + yh].astype(jnp.float32) for n in range(4)
            ]
            for s in range(4):
                at = (yh * 4 + s) * SUB
                rows_ref[at : at + SUB, quad * 128 : quad * 128 + 128] = turned(tiles, s)
    rows = rows_ref[...]
    out_ref[:, : 2 * XF] = rows.astype(jnp.bfloat16)
    square = rows * rows
    high = square.astype(jnp.bfloat16)
    low = (square - high.astype(jnp.float32)).astype(jnp.bfloat16)
    parts = jnp.concatenate(
        [part.astype(jnp.bfloat16) for part in three_parts(noise_ref[...])], axis=0
    )
    sums = lax.dot_general(
        parts, high, NT_DIMS, preferred_element_type=jnp.float32
    ) + lax.dot_general(parts, low, NT_DIMS, preferred_element_type=jnp.float32)
    norms = sums[0:G] + (sums[G : 2 * G] + sums[2 * G : 3 * G])
    small_ref[...] = jnp.zeros_like(small_ref)
    for k, value in enumerate(three_parts(norms)):
        small_ref[k * G : (k + 1) * G, 0:ROWS] = value
    out_ref[:, 2 * XF :] = small_ref[...].T[0:ROWS].astype(jnp.bfloat16)


def product(shifted_ref, block_ref):
    total = None
    for x in range(4):
        part = lax.dot_general(
            shifted_ref[:, x * KX : (x + 1) * KX],
            block_ref[x],
            NT_DIMS,
            preferred_element_type=jnp.float32,
        )
        total = part if total is None else total + part
    return total


def half_kernel(shifted_ref, mine_ref, out_ref):
    out_ref[...] = product(shifted_ref, mine_ref)


def score_kernel(shifted_ref, other_ref, half_ref, chosen_ref, order_ref, out_ref, rest_ref):
    rest_ref[...] = product(shifted_ref, other_ref)
    scores = [
        [from_ref[t * PART : (t + 1) * PART, :] for t in range(NT)]
        for from_ref in (half_ref, rest_ref)
    ]
    tops = [jnp.maximum(jnp.maximum(s[0], s[1]), s[2]) for s in scores]
    peak = jnp.max(jnp.maximum(tops[0], tops[1]), axis=1, keepdims=True)
    raised = sum(jnp.exp(s - peak) for half in scores for s in half)
    log_norm = peak + jnp.log(jnp.sum(raised, axis=1, keepdims=True))
    column = lax.broadcasted_iota(jnp.int32, (PART, 4 * 128), 1)
    ordered = jnp.where((column & 127) == JBLK, log_norm, 0.0)
    for source, half in enumerate(scores):
        posterior = sum(jnp.exp(s - log_norm) for s in half)
        ordered += jnp.dot(
            posterior, order_ref[source], precision=HIGH, preferred_element_type=jnp.float32
        )
    for rank in range(2):
        slots = jnp.dot(
            chosen_ref[rank], ordered, precision=HIGH, preferred_element_type=jnp.float32
        )
        for block in range(4):
            out_ref[block * PART : (block + 1) * PART, rank, :] = slots[
                :, block * 128 : (block + 1) * 128
            ]


def slot_choice(destinations):
    target = destinations[:, 0]
    same = target[:, None] == target[None, :]
    local_index = jnp.arange(PART, dtype=jnp.int32)
    lower = local_index[:, None] > local_index[None, :]
    rank = jnp.sum(jnp.where(same & lower, 1, 0), axis=1)
    slot = jnp.arange(PART, dtype=jnp.int32)[None, :, None]
    ranks = jnp.arange(2, dtype=jnp.int32)[:, None, None]
    chosen = (slot == target[None, None, :]) & (ranks == rank[None, None, :])
    return chosen.astype(jnp.float32)


def column_order():
    core = lax.axis_index("core")
    column = jnp.arange(4 * 128, dtype=jnp.int32)
    block = column // 128
    within = column % 128
    source = jnp.where(block % 2 == core, 0, 1)
    lane = (block // 2) * JBLK + within % 4 * SUB + within // 4
    lane = jnp.where(within < JBLK, lane, -1)
    sources = jnp.arange(2, dtype=jnp.int32)[:, None, None] == source[None, None, :]
    lanes = jnp.arange(ROWS, dtype=jnp.int32)[None, :, None] == lane[None, None, :]
    return (sources & lanes).astype(jnp.float32)


def call(kernel, name, shape, dtype, inputs, scratch=()):
    whole = pl.BlockSpec(memory_space=pltpu.VMEM)
    return pl.pallas_call(
        kernel,
        out_shape=jax.ShapeDtypeStruct(shape, dtype),
        in_specs=[whole] * len(inputs),
        out_specs=whole,
        scratch_shapes=list(scratch),
        name=name,
    )(*inputs)


def shards(images, destinations, group_ids, offsets, inv_noise, ctf_table, references):
    piece = references.reshape(SUB, 128)
    plane = lax.all_to_all(
        jnp.broadcast_to(piece[None], (64, SUB, 128)), ("z", "yl", "yh"), 0, 0, tiled=True
    )

    cosines, sines = phase_tables(offsets)
    noise = by_x(inv_noise)[None, :]
    ctf = by_x(ctf_table)
    group_hot = (group_ids[:, None] == jnp.arange(G, dtype=jnp.int32)[None, :]).astype(jnp.float32)
    lane = jnp.arange(128, dtype=jnp.int32)[None, :]
    minus = jnp.where((lane < 3 * G) & (lane % G == group_ids[:, None]), -0.5, 0.0)
    shifted = call(
        shift_kernel,
        "shift",
        (NT * PART, 4 * KX),
        jnp.bfloat16,
        (images, group_hot, minus, noise, ctf, cosines, sines),
    )
    noise_ctf = noise * ctf * ctf
    own = lax.dynamic_slice_in_dim(noise_ctf, lax.axis_index("x") * XF, XF, 1)
    noise_terms = jnp.concatenate([own, own], axis=1)
    chosen = slot_choice(destinations)
    order = column_order()
    plane, noise_terms, shifted, chosen, order = lax.optimization_barrier(
        (plane, noise_terms, shifted, chosen, order)
    )
    block = call(
        layout_kernel,
        "layout",
        (ROWS, KX),
        jnp.bfloat16,
        (plane, noise_terms),
        (pltpu.VMEM((ROWS, 2 * XF), jnp.float32), pltpu.VMEM((128, 256), jnp.float32)),
    )
    mine = lax.all_to_all(jnp.broadcast_to(block[None], (4, ROWS, KX)), "x", 0, 0, tiled=True)
    other = lax.ppermute(mine, "core", [(0, 1), (1, 0)])
    half = call(half_kernel, "half", (NT * PART, ROWS), jnp.float32, (shifted, mine))
    sends = call(
        score_kernel,
        "score",
        (4 * PART, 2, 128),
        jnp.float32,
        (shifted, other, half, chosen, order),
        (pltpu.VMEM((NT * PART, ROWS), jnp.float32),),
    )
    whole = lax.all_to_all(sends, CLS + DOM, 0, 0, tiled=True).reshape(8 * PART, 128)
    return (whole[:, :JBLK], whole[:, JBLK])


def solution(mesh):
    split = Mesh(mesh.devices.reshape(8, 4, 4, 2, 2), SPLIT_AXES)
    return jax.shard_map(
        shards,
        mesh=split,
        in_specs=(
            P(SPLIT_AXES, None),
            P(SPLIT_AXES, None),
            P(SPLIT_AXES),
            P(),
            P(),
            P(),
            P(CLS, DOM),
        ),
        out_specs=(P(DOM, CLS), P(DOM)),
        check_vma=False,
    )
```

```python
import math

import jax
import jax.numpy as jnp
from jax import lax
from jax.experimental import pallas as pl
from jax.experimental.pallas import tpu as pltpu
from jax.sharding import Mesh
from jax.sharding import PartitionSpec as P

SIDE = 64
F = 2048
NT = 3
G = 16
PART = 128
JBLK = 72
SUB = 18
ROWS = 2 * JBLK
XF = F // 4
KX = 2 * XF + 128
SPLIT_AXES = ("z", "yl", "x", "yh", "core")
DOM = ("z", "yl", "x")
CLS = ("yh", "core")
HIGH = lax.Precision.HIGHEST
NT_DIMS = (((1,), (1,)), ((), ()))


def by_x(values):
    split = values.reshape(values.shape[:-1] + (16, 4, 32))
    return jnp.moveaxis(split, -2, -3).reshape(values.shape)


def phase_tables(offsets):
    place = jnp.arange(F, dtype=jnp.int32)
    freq_index = (place % XF) // 32 * 128 + place // XF * 32 + place % 32
    half_side = SIDE // 2
    row_freq = freq_index // half_side
    col_freq = freq_index % half_side
    row_freq = jnp.where(row_freq >= half_side, row_freq - SIDE, row_freq)
    turns = jnp.mod(offsets[:, 0:1] * row_freq[None, :] + offsets[:, 1:2] * col_freq[None, :], SIDE)
    angles = turns.astype(jnp.float32) * (2.0 * math.pi / SIDE)
    return (jnp.cos(angles), jnp.sin(angles))


def three_parts(value):
    first = value.astype(jnp.bfloat16).astype(jnp.float32)
    rest = value - first
    second = rest.astype(jnp.bfloat16).astype(jnp.float32)
    return (first, second, rest - second)


def turned(tiles, x):
    return jnp.concatenate([tile[:, x * 32 : x * 32 + 32] for tile in tiles], axis=1)


def shift_kernel(images_ref, hot_ref, minus_ref, noise_ref, ctf_ref, cos_ref, sin_ref, out_ref):
    for quad in range(4):
        real_tiles, imag_tiles = (
            [
                images_ref[:, start + n * 128 : start + n * 128 + 128].astype(jnp.float32)
                for n in range(4)
            ]
            for start in (quad * 512, F + quad * 512)
        )
        for x in range(4):
            cols = slice(x * XF + quad * 128, x * XF + quad * 128 + 128)
            real_part = turned(real_tiles, x)
            imag_part = turned(imag_tiles, x)
            ctf_rows = jnp.dot(
                hot_ref[...], ctf_ref[:, cols], precision=HIGH, preferred_element_type=jnp.float32
            )
            weight = noise_ref[:, cols] * ctf_rows
            at = x * KX + quad * 128
            for t in range(NT):
                cosine = cos_ref[t : t + 1, cols]
                sine = sin_ref[t : t + 1, cols]
                rows = slice(t * PART, (t + 1) * PART)
                out_ref[rows, at : at + 128] = (
                    weight * (real_part * cosine - imag_part * sine)
                ).astype(jnp.bfloat16)
                out_ref[rows, at + XF : at + XF + 128] = (
                    weight * (real_part * sine + imag_part * cosine)
                ).astype(jnp.bfloat16)
    for x in range(4):
        for t in range(NT):
            out_ref[t * PART : (t + 1) * PART, x * KX + 2 * XF : (x + 1) * KX] = minus_ref[
                ...
            ].astype(jnp.bfloat16)


def layout_kernel(plane_ref, noise_ref, out_ref, rows_ref, small_ref):
    for yh in range(2):
        for quad in range(8):
            tiles = [
                plane_ref[(quad * 4 + n) * 2 + yh].astype(jnp.float32) for n in range(4)
            ]
            for s in range(4):
                at = (yh * 4 + s) * SUB
                rows_ref[at : at + SUB, quad * 128 : quad * 128 + 128] = turned(tiles, s)
    rows = rows_ref[...]
    out_ref[:, : 2 * XF] = rows.astype(jnp.bfloat16)
    square = rows * rows
    high = square.astype(jnp.bfloat16)
    low = (square - high.astype(jnp.float32)).astype(jnp.bfloat16)
    parts = jnp.concatenate(
        [part.astype(jnp.bfloat16) for part in three_parts(noise_ref[...])], axis=0
    )
    sums = lax.dot_general(
        parts, high, NT_DIMS, preferred_element_type=jnp.float32
    ) + lax.dot_general(parts, low, NT_DIMS, preferred_element_type=jnp.float32)
    norms = sums[0:G] + (sums[G : 2 * G] + sums[2 * G : 3 * G])
    small_ref[...] = jnp.zeros_like(small_ref)
    for k, value in enumerate(three_parts(norms)):
        small_ref[k * G : (k + 1) * G, 0:ROWS] = value
    out_ref[:, 2 * XF :] = small_ref[...].T[0:ROWS].astype(jnp.bfloat16)


def product(shifted_ref, block_ref):
    total = None
    for x in range(4):
        part = lax.dot_general(
            shifted_ref[:, x * KX : (x + 1) * KX],
            block_ref[x],
            NT_DIMS,
            preferred_element_type=jnp.float32,
        )
        total = part if total is None else total + part
    return total


def half_kernel(shifted_ref, mine_ref, out_ref):
    out_ref[...] = product(shifted_ref, mine_ref)


def score_kernel(shifted_ref, other_ref, half_ref, chosen_ref, order_ref, out_ref, rest_ref):
    rest_ref[...] = product(shifted_ref, other_ref)
    scores = [
        [from_ref[t * PART : (t + 1) * PART, :] for t in range(NT)]
        for from_ref in (half_ref, rest_ref)
    ]
    tops = [jnp.maximum(jnp.maximum(s[0], s[1]), s[2]) for s in scores]
    peak = jnp.max(jnp.maximum(tops[0], tops[1]), axis=1, keepdims=True)
    raised = sum(jnp.exp(s - peak) for half in scores for s in half)
    log_norm = peak + jnp.log(jnp.sum(raised, axis=1, keepdims=True))
    column = lax.broadcasted_iota(jnp.int32, (PART, 4 * 128), 1)
    ordered = jnp.where((column & 127) == JBLK, log_norm, 0.0)
    for source, half in enumerate(scores):
        posterior = sum(jnp.exp(s - log_norm) for s in half)
        ordered += selected(posterior, order_ref[source])
    first, second, third = (
        jnp.dot(chosen_ref[...], part.astype(jnp.bfloat16), preferred_element_type=jnp.float32)
        for part in three_parts(ordered)
    )
    slots = first + (second + third)
    for block in range(4):
        out_ref[block * 2 * PART : (block + 1) * 2 * PART, :] = slots[
            :, block * 128 : (block + 1) * 128
        ]


def selected(values, one_hot):
    parts = jnp.concatenate([part.astype(jnp.bfloat16) for part in three_parts(values)], axis=0)
    each = jnp.dot(parts, one_hot, preferred_element_type=jnp.float32)
    count = values.shape[0]
    return each[0:count] + (each[count : 2 * count] + each[2 * count :])


def slot_choice(destinations):
    target = destinations[:, 0]
    same = target[:, None] == target[None, :]
    local_index = jnp.arange(PART, dtype=jnp.int32)
    lower = local_index[:, None] > local_index[None, :]
    rank = jnp.sum(jnp.where(same & lower, 1, 0), axis=1)
    slot_of = target * 2 + rank
    slots = jnp.arange(2 * PART, dtype=jnp.int32)
    return (slots[:, None] == slot_of[None, :]).astype(jnp.bfloat16)


def column_order():
    core = lax.axis_index("core")
    column = jnp.arange(4 * 128, dtype=jnp.int32)
    block = column // 128
    within = column % 128
    source = jnp.where(block % 2 == core, 0, 1)
    lane = (block // 2) * JBLK + within % 4 * SUB + within // 4
    lane = jnp.where(within < JBLK, lane, -1)
    sources = jnp.arange(2, dtype=jnp.int32)[:, None, None] == source[None, None, :]
    lanes = jnp.arange(ROWS, dtype=jnp.int32)[None, :, None] == lane[None, None, :]
    return (sources & lanes).astype(jnp.bfloat16)


def call(kernel, name, shape, dtype, inputs, scratch=()):
    whole = pl.BlockSpec(memory_space=pltpu.VMEM)
    return pl.pallas_call(
        kernel,
        out_shape=jax.ShapeDtypeStruct(shape, dtype),
        in_specs=[whole] * len(inputs),
        out_specs=whole,
        scratch_shapes=list(scratch),
        compiler_params=pltpu.CompilerParams(vmem_limit_bytes=24 * 1024 * 1024),
        name=name,
    )(*inputs)


def shards(images, destinations, group_ids, offsets, inv_noise, ctf_table, references):
    piece = references.reshape(SUB, 128)
    plane = lax.all_to_all(
        jnp.broadcast_to(piece[None], (64, SUB, 128)), ("z", "yl", "yh"), 0, 0, tiled=True
    )

    cosines, sines = phase_tables(offsets)
    noise = by_x(inv_noise)[None, :]
    ctf = by_x(ctf_table)
    group_hot = (group_ids[:, None] == jnp.arange(G, dtype=jnp.int32)[None, :]).astype(jnp.float32)
    lane = jnp.arange(128, dtype=jnp.int32)[None, :]
    minus = jnp.where((lane < 3 * G) & (lane % G == group_ids[:, None]), -0.5, 0.0)
    shifted = call(
        shift_kernel,
        "shift",
        (NT * PART, 4 * KX),
        jnp.bfloat16,
        (images, group_hot, minus, noise, ctf, cosines, sines),
    )
    noise_ctf = noise * ctf * ctf
    own = lax.dynamic_slice_in_dim(noise_ctf, lax.axis_index("x") * XF, XF, 1)
    noise_terms = jnp.concatenate([own, own], axis=1)
    chosen = slot_choice(destinations)
    order = column_order()
    plane, noise_terms, shifted, chosen, order = lax.optimization_barrier(
        (plane, noise_terms, shifted, chosen, order)
    )
    block = call(
        layout_kernel,
        "layout",
        (ROWS, KX),
        jnp.bfloat16,
        (plane, noise_terms),
        (pltpu.VMEM((ROWS, 2 * XF), jnp.float32), pltpu.VMEM((128, 256), jnp.float32)),
    )
    mine = lax.all_to_all(jnp.broadcast_to(block[None], (4, ROWS, KX)), "x", 0, 0, tiled=True)
    other = lax.ppermute(mine, "core", [(0, 1), (1, 0)])
    half = call(half_kernel, "half", (NT * PART, ROWS), jnp.float32, (shifted, mine))
    sends = call(
        score_kernel,
        "score",
        (8 * PART, 128),
        jnp.float32,
        (shifted, other, half, chosen, order),
        (pltpu.VMEM((NT * PART, ROWS), jnp.float32),),
    )
    whole = lax.all_to_all(sends.reshape(4 * PART, 2, 128), CLS + DOM, 0, 0, tiled=True).reshape(8 * PART, 128)
    return (whole[:, :JBLK], whole[:, JBLK])


def solution(mesh):
    split = Mesh(mesh.devices.reshape(8, 4, 4, 2, 2), SPLIT_AXES)
    return jax.shard_map(
        shards,
        mesh=split,
        in_specs=(
            P(SPLIT_AXES, None),
            P(SPLIT_AXES, None),
            P(SPLIT_AXES),
            P(),
            P(),
            P(),
            P(CLS, DOM),
        ),
        out_specs=(P(DOM, CLS), P(DOM)),
        check_vma=False,
    )
```

```python
import math

import jax
import jax.numpy as jnp
from jax import lax
from jax.experimental import pallas as pl
from jax.experimental.pallas import tpu as pltpu
from jax.sharding import Mesh
from jax.sharding import PartitionSpec as P

SIDE = 64
F = 2048
NT = 3
G = 16
PART = 128
JBLK = 72
SUB = 18
ROWS = 2 * JBLK
XF = F // 4
KX = 2 * XF + 128
SPLIT_AXES = ("z", "yl", "x", "yh", "core")
DOM = ("z", "yl", "x")
CLS = ("yh", "core")
HIGH = lax.Precision.HIGHEST
NT_DIMS = (((1,), (1,)), ((), ()))


def phase_tables(offsets):
    freq_index = jnp.arange(F, dtype=jnp.int32)
    half_side = SIDE // 2
    row_freq = freq_index // half_side
    col_freq = freq_index % half_side
    row_freq = jnp.where(row_freq >= half_side, row_freq - SIDE, row_freq)
    turns = jnp.mod(offsets[:, 0:1] * row_freq[None, :] + offsets[:, 1:2] * col_freq[None, :], SIDE)
    angles = turns.astype(jnp.float32) * (2.0 * math.pi / SIDE)
    return (jnp.cos(angles), jnp.sin(angles))


def three_parts(value):
    first = value.astype(jnp.bfloat16).astype(jnp.float32)
    rest = value - first
    second = rest.astype(jnp.bfloat16).astype(jnp.float32)
    return (first, second, rest - second)


def turned(tiles, x):
    return jnp.concatenate([tile[:, x * 32 : x * 32 + 32] for tile in tiles], axis=1)


def shift_kernel(place_ref, images_ref, groups_ref, noise_ref, ctf_ref, cos_ref, sin_ref, out_ref):
    row = lax.broadcasted_iota(jnp.int32, (128, PART), 0)
    hot = jnp.where((row < 3 * G) & ((row & (G - 1)) == groups_ref[...]), 1.0, 0.0).T
    hot_parts = hot.astype(jnp.bfloat16)
    empty = jnp.zeros((128 - 3 * G, 128), jnp.bfloat16)
    own_terms = []
    for quad in range(4):
        real_tiles, imag_tiles = (tiles_of(images_ref, start) for start in (quad * 512, F + quad * 512))
        noise_tiles, ctf_tiles, cos_tiles, sin_tiles = (
            tiles_of(ref, quad * 512) for ref in (noise_ref, ctf_ref, cos_ref, sin_ref)
        )
        own = [turned(ref_tiles, 0) for ref_tiles in (noise_tiles, ctf_tiles)]
        for x in range(1, 4):
            here = place_ref[0] == x
            own[0] = jnp.where(here, turned(noise_tiles, x), own[0])
            own[1] = jnp.where(here, turned(ctf_tiles, x), own[1])
        own_terms.append(own[0] * own[1] * own[1])
        for x in range(4):
            real_part = turned(real_tiles, x)
            imag_part = turned(imag_tiles, x)
            noise = turned(noise_tiles, x)
            ctf = turned(ctf_tiles, x)
            cosines = turned(cos_tiles, x)
            sines = turned(sin_tiles, x)
            ctf_parts = jnp.concatenate(
                [part.astype(jnp.bfloat16) for part in three_parts(ctf)] + [empty], axis=0
            )
            weight = noise * jnp.dot(hot_parts, ctf_parts, preferred_element_type=jnp.float32)
            at = x * KX + quad * 128
            for t in range(NT):
                cosine = cosines[t : t + 1]
                sine = sines[t : t + 1]
                rows = slice(t * PART, (t + 1) * PART)
                out_ref[rows, at : at + 128] = (
                    weight * (real_part * cosine - imag_part * sine)
                ).astype(jnp.bfloat16)
                out_ref[rows, at + XF : at + XF + 128] = (
                    weight * (real_part * sine + imag_part * cosine)
                ).astype(jnp.bfloat16)
    minus = (-0.5 * hot).astype(jnp.bfloat16)
    for x in range(4):
        for t in range(NT):
            out_ref[t * PART : (t + 1) * PART, x * KX + 2 * XF : (x + 1) * KX] = minus
    for quad, term in enumerate(own_terms):
        for k, part in enumerate(three_parts(term)):
            for half in range(2):
                row, column = spare_place(quad * 2 + half)
                out_ref[row + k * G : row + (k + 1) * G, column : column + 64] = part[
                    :, half * 64 : half * 64 + 64
                ].astype(jnp.bfloat16)


def spare_place(n):
    return (n // 4 * 3 * G, n % 4 * KX + 2 * XF + 64)


def tiles_of(ref, start):
    return [
        ref[:, start + n * 128 : start + n * 128 + 128].astype(jnp.float32) for n in range(4)
    ]


def layout_kernel(plane_ref, shifted_ref, out_ref, rows_ref, small_ref):
    for yh in range(2):
        for quad in range(8):
            tiles = [
                plane_ref[(quad * 4 + n) * 2 + yh].astype(jnp.float32) for n in range(4)
            ]
            for s in range(4):
                at = (yh * 4 + s) * SUB
                rows_ref[at : at + SUB, quad * 128 : quad * 128 + 128] = turned(tiles, s)
    rows = rows_ref[...]
    out_ref[:, : 2 * XF] = rows.astype(jnp.bfloat16)
    square = rows * rows
    high = square.astype(jnp.bfloat16)
    low = (square - high.astype(jnp.float32)).astype(jnp.bfloat16)
    pieces = []
    for n in range(8):
        row, column = spare_place(n)
        pieces.append(shifted_ref[row : row + 3 * G, column : column + 64])
    parts = jnp.concatenate(pieces, axis=1)
    parts = jnp.concatenate([parts, parts], axis=1)
    sums = lax.dot_general(
        parts, high, NT_DIMS, preferred_element_type=jnp.float32
    ) + lax.dot_general(parts, low, NT_DIMS, preferred_element_type=jnp.float32)
    norms = sums[0:G] + (sums[G : 2 * G] + sums[2 * G : 3 * G])
    small_ref[...] = jnp.zeros_like(small_ref)
    for k, value in enumerate(three_parts(norms)):
        small_ref[k * G : (k + 1) * G, 0:ROWS] = value
    out_ref[:, 2 * XF :] = small_ref[...].T[0:ROWS].astype(jnp.bfloat16)


def product(shifted_ref, block_ref):
    total = None
    for x in range(4):
        part = lax.dot_general(
            shifted_ref[:, x * KX : (x + 1) * KX],
            block_ref[x],
            NT_DIMS,
            preferred_element_type=jnp.float32,
        )
        total = part if total is None else total + part
    return total


def half_kernel(place_ref, shifted_ref, mine_ref, target_ref, out_ref, chosen_ref, order_ref):
    out_ref[...] = product(shifted_ref, mine_ref)
    target = jnp.broadcast_to(target_ref[...].astype(jnp.float32), (PART, PART))
    row = lax.broadcasted_iota(jnp.int32, (PART, PART), 0)
    column = lax.broadcasted_iota(jnp.int32, (PART, PART), 1)
    earlier = jnp.where((target == target.T) & (row < column), 1.0, 0.0)
    slot_of = 2.0 * target[0:1] + jnp.sum(earlier, axis=0, keepdims=True)
    slot = lax.broadcasted_iota(jnp.int32, (2 * PART, PART), 0).astype(jnp.float32)
    chosen_ref[...] = jnp.where(slot == slot_of, 1.0, 0.0).astype(jnp.bfloat16)
    column = lax.broadcasted_iota(jnp.int32, (ROWS, 4 * 128), 1)
    lane = lax.broadcasted_iota(jnp.int32, (ROWS, 4 * 128), 0)
    block = column >> 7
    within = column & 127
    wanted = (block >> 1) * JBLK + (within & 3) * SUB + (within >> 2)
    kept = (within < JBLK) & (wanted == lane)
    for source in range(2):
        from_it = ((block & 1) ^ place_ref[1]) == source
        order_ref[source] = jnp.where(kept & from_it, 1.0, 0.0).astype(jnp.bfloat16)


def score_kernel(shifted_ref, other_ref, half_ref, chosen_ref, order_ref, out_ref, rest_ref):
    rest_ref[...] = product(shifted_ref, other_ref)
    scores = [
        [from_ref[t * PART : (t + 1) * PART, :] for t in range(NT)]
        for from_ref in (half_ref, rest_ref)
    ]
    tops = [jnp.maximum(jnp.maximum(s[0], s[1]), s[2]) for s in scores]
    peak = jnp.max(jnp.maximum(tops[0], tops[1]), axis=1, keepdims=True)
    raised = sum(jnp.exp(s - peak) for half in scores for s in half)
    log_norm = peak + jnp.log(jnp.sum(raised, axis=1, keepdims=True))
    column = lax.broadcasted_iota(jnp.int32, (PART, 4 * 128), 1)
    ordered = jnp.where((column & 127) == JBLK, log_norm, 0.0)
    for source, half in enumerate(scores):
        posterior = sum(jnp.exp(s - log_norm) for s in half)
        ordered += selected(posterior, order_ref[source])
    first, second, third = (
        jnp.dot(chosen_ref[...], part.astype(jnp.bfloat16), preferred_element_type=jnp.float32)
        for part in three_parts(ordered)
    )
    slots = first + (second + third)
    for block in range(4):
        out_ref[block * 2 * PART : (block + 1) * 2 * PART, :] = slots[
            :, block * 128 : (block + 1) * 128
        ]


def selected(values, one_hot):
    parts = jnp.concatenate([part.astype(jnp.bfloat16) for part in three_parts(values)], axis=0)
    each = jnp.dot(parts, one_hot, preferred_element_type=jnp.float32)
    count = values.shape[0]
    return each[0:count] + (each[count : 2 * count] + each[2 * count :])


def call(kernel, name, outs, inputs, scratch=(), scalars=0):
    whole = pl.BlockSpec(memory_space=pltpu.VMEM)
    numbers = pl.BlockSpec(memory_space=pltpu.SMEM)
    shapes = [jax.ShapeDtypeStruct(shape, dtype) for shape, dtype in outs]
    results = pl.pallas_call(
        kernel,
        out_shape=shapes,
        in_specs=[numbers] * scalars + [whole] * (len(inputs) - scalars),
        out_specs=[whole] * len(outs),
        scratch_shapes=list(scratch),
        compiler_params=pltpu.CompilerParams(vmem_limit_bytes=24 * 1024 * 1024),
        name=name,
    )(*inputs)
    return results


def shards(images, destinations, group_ids, offsets, inv_noise, ctf_table, references):
    f32, bf16 = jnp.float32, jnp.bfloat16
    piece = references.reshape(SUB, 128)
    plane = lax.all_to_all(
        jnp.broadcast_to(piece[None], (64, SUB, 128)), ("z", "yl", "yh"), 0, 0, tiled=True
    )
    place = jnp.stack([lax.axis_index("x"), lax.axis_index("core")]).astype(jnp.int32)
    cosines, sines = phase_tables(offsets)
    (shifted,) = call(
        shift_kernel,
        "shift",
        [((NT * PART, 4 * KX), bf16)],
        (place, images, group_ids[None, :], inv_noise[None, :], ctf_table, cosines, sines),
        scalars=1,
    )
    plane, shifted, place = lax.optimization_barrier((plane, shifted, place))
    (block,) = call(
        layout_kernel,
        "layout",
        [((ROWS, KX), bf16)],
        (plane, shifted),
        (pltpu.VMEM((ROWS, 2 * XF), f32), pltpu.VMEM((128, 256), f32)),
    )
    mine = lax.all_to_all(jnp.broadcast_to(block[None], (4, ROWS, KX)), "x", 0, 0, tiled=True)
    other = lax.ppermute(mine, "core", [(0, 1), (1, 0)])
    half, chosen, order = call(
        half_kernel,
        "half",
        [((NT * PART, ROWS), f32), ((2 * PART, PART), bf16), ((2, ROWS, 4 * 128), bf16)],
        (place, shifted, mine, destinations.reshape(1, PART)),
        scalars=1,
    )
    (sends,) = call(
        score_kernel,
        "score",
        [((8 * PART, 128), f32)],
        (shifted, other, half, chosen, order),
        (pltpu.VMEM((NT * PART, ROWS), f32),),
    )
    whole = lax.all_to_all(sends.reshape(4 * PART, 2, 128), CLS + DOM, 0, 0, tiled=True)
    whole = whole.reshape(8 * PART, 128)
    return (whole[:, :JBLK], whole[:, JBLK])


def solution(mesh):
    split = Mesh(mesh.devices.reshape(8, 4, 4, 2, 2), SPLIT_AXES)
    return jax.shard_map(
        shards,
        mesh=split,
        in_specs=(
            P(SPLIT_AXES, None),
            P(SPLIT_AXES, None),
            P(SPLIT_AXES),
            P(),
            P(),
            P(),
            P(CLS, DOM),
        ),
        out_specs=(P(DOM, CLS), P(DOM)),
        check_vma=False,
    )
```

```python
import math

import jax
import jax.numpy as jnp
from jax import lax
from jax.experimental import pallas as pl
from jax.experimental.pallas import tpu as pltpu
from jax.sharding import Mesh
from jax.sharding import PartitionSpec as P

SIDE = 64
F = 2048
NT = 3
G = 16
PART = 128
JBLK = 72
SUB = 18
ROWS = 2 * JBLK
XF = F // 4
KX = 2 * XF + 128
SCALE = 32768.0
SPLIT_AXES = ("z", "yl", "x", "yh", "core")
DOM = ("z", "yl", "x")
CLS = ("yh", "core")
HIGH = lax.Precision.HIGHEST
NT_DIMS = (((1,), (1,)), ((), ()))


def phase_tables(offsets):
    freq_index = jnp.arange(F, dtype=jnp.int32)
    half_side = SIDE // 2
    row_freq = freq_index // half_side
    col_freq = freq_index % half_side
    row_freq = jnp.where(row_freq >= half_side, row_freq - SIDE, row_freq)
    turns = jnp.mod(offsets[:, 0:1] * row_freq[None, :] + offsets[:, 1:2] * col_freq[None, :], SIDE)
    angles = turns.astype(jnp.float32) * (2.0 * math.pi / SIDE)
    return (jnp.cos(angles), jnp.sin(angles))


def three_parts(value):
    first = value.astype(jnp.bfloat16).astype(jnp.float32)
    rest = value - first
    second = rest.astype(jnp.bfloat16).astype(jnp.float32)
    return (first, second, rest - second)


def turned(tiles, x):
    return jnp.concatenate([tile[:, x * 32 : x * 32 + 32] for tile in tiles], axis=1)


def shift_kernel(place_ref, images_ref, groups_ref, noise_ref, ctf_ref, cos_ref, sin_ref, out_ref):
    row = lax.broadcasted_iota(jnp.int32, (128, PART), 0)
    hot = jnp.where((row < 3 * G) & ((row & (G - 1)) == groups_ref[...]), 1.0, 0.0).T
    hot_parts = hot.astype(jnp.bfloat16)
    empty = jnp.zeros((128 - 3 * G, 128), jnp.bfloat16)
    own_terms = []
    for quad in range(4):
        real_tiles, imag_tiles = (tiles_of(images_ref, start) for start in (quad * 512, F + quad * 512))
        noise_tiles, ctf_tiles, cos_tiles, sin_tiles = (
            tiles_of(ref, quad * 512) for ref in (noise_ref, ctf_ref, cos_ref, sin_ref)
        )
        own = [turned(ref_tiles, 0) for ref_tiles in (noise_tiles, ctf_tiles)]
        for x in range(1, 4):
            here = place_ref[0] == x
            own[0] = jnp.where(here, turned(noise_tiles, x), own[0])
            own[1] = jnp.where(here, turned(ctf_tiles, x), own[1])
        own_terms.append(own[0] * own[1] * own[1])
        for x in range(4):
            real_part = turned(real_tiles, x)
            imag_part = turned(imag_tiles, x)
            noise = turned(noise_tiles, x)
            ctf = turned(ctf_tiles, x)
            cosines = turned(cos_tiles, x)
            sines = turned(sin_tiles, x)
            ctf_parts = jnp.concatenate(
                [part.astype(jnp.bfloat16) for part in three_parts(ctf)] + [empty], axis=0
            )
            weight = noise * jnp.dot(hot_parts, ctf_parts, preferred_element_type=jnp.float32)
            at = x * KX + quad * 128
            for t in range(NT):
                cosine = cosines[t : t + 1]
                sine = sines[t : t + 1]
                rows = slice(t * PART, (t + 1) * PART)
                out_ref[rows, at : at + 128] = (
                    weight * (real_part * cosine - imag_part * sine)
                ).astype(jnp.bfloat16)
                out_ref[rows, at + XF : at + XF + 128] = (
                    weight * (real_part * sine + imag_part * cosine)
                ).astype(jnp.bfloat16)
    minus = (-0.5 * hot).astype(jnp.bfloat16)
    for x in range(4):
        for t in range(NT):
            out_ref[t * PART : (t + 1) * PART, x * KX + 2 * XF : (x + 1) * KX] = minus
    for quad, term in enumerate(own_terms):
        for k, part in enumerate(three_parts(term)):
            for half in range(2):
                row, column = spare_place(quad * 2 + half)
                out_ref[row + k * G : row + (k + 1) * G, column : column + 64] = part[
                    :, half * 64 : half * 64 + 64
                ].astype(jnp.bfloat16)


def spare_place(n):
    return (n // 4 * 3 * G, n % 4 * KX + 2 * XF + 64)


def tiles_of(ref, start):
    return [
        ref[:, start + n * 128 : start + n * 128 + 128].astype(jnp.float32) for n in range(4)
    ]


def layout_kernel(plane_ref, shifted_ref, out_ref, rows_ref, small_ref):
    for yh in range(2):
        for quad in range(8):
            tiles = [
                plane_ref[(quad * 4 + n) * 2 + yh].astype(jnp.float32) for n in range(4)
            ]
            for s in range(4):
                at = (yh * 4 + s) * SUB
                rows_ref[at : at + SUB, quad * 128 : quad * 128 + 128] = turned(tiles, s)
    rows = rows_ref[...]
    out_ref[:, : 2 * XF] = rows.astype(jnp.bfloat16)
    square = rows * rows
    high = square.astype(jnp.bfloat16)
    low = (square - high.astype(jnp.float32)).astype(jnp.bfloat16)
    pieces = []
    for n in range(8):
        row, column = spare_place(n)
        pieces.append(shifted_ref[row : row + 3 * G, column : column + 64])
    parts = jnp.concatenate(pieces, axis=1)
    parts = jnp.concatenate([parts, parts], axis=1)
    sums = lax.dot_general(
        parts, high, NT_DIMS, preferred_element_type=jnp.float32
    ) + lax.dot_general(parts, low, NT_DIMS, preferred_element_type=jnp.float32)
    norms = sums[0:G] + (sums[G : 2 * G] + sums[2 * G : 3 * G])
    small_ref[...] = jnp.zeros_like(small_ref)
    for k, value in enumerate(three_parts(norms)):
        small_ref[k * G : (k + 1) * G, 0:ROWS] = value
    out_ref[:, 2 * XF :] = small_ref[...].T[0:ROWS].astype(jnp.bfloat16)


def product(shifted_ref, block_ref):
    total = None
    for x in range(4):
        part = lax.dot_general(
            shifted_ref[:, x * KX : (x + 1) * KX],
            block_ref[x],
            NT_DIMS,
            preferred_element_type=jnp.float32,
        )
        total = part if total is None else total + part
    return total


def half_kernel(place_ref, shifted_ref, mine_ref, target_ref, out_ref, chosen_ref, order_ref):
    out_ref[...] = product(shifted_ref, mine_ref)
    target = jnp.broadcast_to(target_ref[...].astype(jnp.float32), (PART, PART))
    row = lax.broadcasted_iota(jnp.int32, (PART, PART), 0)
    column = lax.broadcasted_iota(jnp.int32, (PART, PART), 1)
    earlier = jnp.where((target == target.T) & (row < column), 1.0, 0.0)
    slot_of = 2.0 * target[0:1] + jnp.sum(earlier, axis=0, keepdims=True)
    slot = lax.broadcasted_iota(jnp.int32, (2 * PART, PART), 0).astype(jnp.float32)
    chosen_ref[...] = jnp.where(slot == slot_of, 1.0, 0.0).astype(jnp.bfloat16)
    column = lax.broadcasted_iota(jnp.int32, (ROWS, 4 * 128), 1)
    lane = lax.broadcasted_iota(jnp.int32, (ROWS, 4 * 128), 0)
    block = column >> 7
    within = column & 127
    wanted = (block >> 1) * JBLK + (within & 3) * SUB + (within >> 2)
    kept = (within < JBLK) & (wanted == lane)
    for source in range(2):
        from_it = ((block & 1) ^ place_ref[1]) == source
        order_ref[source] = jnp.where(kept & from_it, 1.0, 0.0).astype(jnp.bfloat16)


def score_kernel(shifted_ref, other_ref, half_ref, chosen_ref, order_ref, out_ref, rest_ref):
    rest_ref[...] = product(shifted_ref, other_ref)
    scores = [
        [from_ref[t * PART : (t + 1) * PART, :] for t in range(NT)]
        for from_ref in (half_ref, rest_ref)
    ]
    tops = [jnp.maximum(jnp.maximum(s[0], s[1]), s[2]) for s in scores]
    peak = jnp.max(jnp.maximum(tops[0], tops[1]), axis=1, keepdims=True)
    raised = sum(jnp.exp(s - peak) for half in scores for s in half)
    log_norm = peak + jnp.log(jnp.sum(raised, axis=1, keepdims=True))
    column = lax.broadcasted_iota(jnp.int32, (PART, 4 * 128), 1)
    within = column & 127
    ordered = jnp.zeros((PART, 4 * 128), jnp.float32)
    for k, piece in enumerate(pieces_of(log_norm)):
        ordered = jnp.where(within == JBLK + k, piece, ordered)
    for source, half in enumerate(scores):
        posterior = SCALE * sum(jnp.exp(s - log_norm) for s in half)
        ordered += selected(posterior, order_ref[source])
    first, second, third = (
        jnp.dot(chosen_ref[...], part.astype(jnp.bfloat16), preferred_element_type=jnp.float32)
        for part in three_parts(ordered)
    )
    slots = first + (second + third)
    for block in range(4):
        out_ref[block * 2 * PART : (block + 1) * 2 * PART, :] = slots[
            :, block * 128 : (block + 1) * 128
        ]


def pieces_of(value):
    thousands = jnp.floor(value * (1.0 / 1024.0) + 0.5)
    rest = value - 1024.0 * thousands
    ones = jnp.floor(rest + 0.5)
    rest = (rest - ones) * 2048.0
    parts = jnp.floor(rest + 0.5)
    return (thousands, ones, parts, rest - parts)


def selected(values, one_hot):
    parts = jnp.concatenate([part.astype(jnp.bfloat16) for part in three_parts(values)], axis=0)
    each = jnp.dot(parts, one_hot, preferred_element_type=jnp.float32)
    count = values.shape[0]
    return each[0:count] + (each[count : 2 * count] + each[2 * count :])


def finish_kernel(slots_ref, posteriors_ref, log_norms_ref):
    rows = slots_ref[...].T
    posteriors_ref[...] = rows[0:JBLK] * (1.0 / SCALE)
    thousands, ones, parts, rest = (rows[JBLK + k : JBLK + k + 1] for k in range(4))
    log_norms_ref[...] = 1024.0 * thousands + (ones + (parts + rest) * (1.0 / 2048.0))


def call(kernel, name, outs, inputs, scratch=(), scalars=0):
    whole = pl.BlockSpec(memory_space=pltpu.VMEM)
    numbers = pl.BlockSpec(memory_space=pltpu.SMEM)
    shapes = [jax.ShapeDtypeStruct(shape, dtype) for shape, dtype in outs]
    results = pl.pallas_call(
        kernel,
        out_shape=shapes,
        in_specs=[numbers] * scalars + [whole] * (len(inputs) - scalars),
        out_specs=[whole] * len(outs),
        scratch_shapes=list(scratch),
        compiler_params=pltpu.CompilerParams(vmem_limit_bytes=24 * 1024 * 1024),
        name=name,
    )(*inputs)
    return results


def shards(images, destinations, group_ids, offsets, inv_noise, ctf_table, references):
    f32, bf16 = jnp.float32, jnp.bfloat16
    piece = references.reshape(SUB, 128)
    plane = lax.all_to_all(
        jnp.broadcast_to(piece[None], (64, SUB, 128)), ("z", "yl", "yh"), 0, 0, tiled=True
    )
    place = jnp.stack([lax.axis_index("x"), lax.axis_index("core")]).astype(jnp.int32)
    cosines, sines = phase_tables(offsets)
    (shifted,) = call(
        shift_kernel,
        "shift",
        [((NT * PART, 4 * KX), bf16)],
        (place, images, group_ids[None, :], inv_noise[None, :], ctf_table, cosines, sines),
        scalars=1,
    )
    plane, shifted, place = lax.optimization_barrier((plane, shifted, place))
    (block,) = call(
        layout_kernel,
        "layout",
        [((ROWS, KX), bf16)],
        (plane, shifted),
        (pltpu.VMEM((ROWS, 2 * XF), f32), pltpu.VMEM((128, 256), f32)),
    )
    mine = lax.all_to_all(jnp.broadcast_to(block[None], (4, ROWS, KX)), "x", 0, 0, tiled=True)
    other = lax.ppermute(mine, "core", [(0, 1), (1, 0)])
    half, chosen, order = call(
        half_kernel,
        "half",
        [((NT * PART, ROWS), f32), ((2 * PART, PART), bf16), ((2, ROWS, 4 * 128), bf16)],
        (place, shifted, mine, destinations.reshape(1, PART)),
        scalars=1,
    )
    (sends,) = call(
        score_kernel,
        "score",
        [((8 * PART, 128), f32)],
        (shifted, other, half, chosen, order),
        (pltpu.VMEM((NT * PART, ROWS), f32),),
    )
    sends = sends.astype(jnp.float16).reshape(4 * PART, 2, 128)
    whole = lax.all_to_all(sends, CLS + DOM, 0, 0, tiled=True)
    posteriors, log_norms = call(
        finish_kernel,
        "finish",
        [((JBLK, 8 * PART), f32), ((1, 8 * PART), f32)],
        (whole.reshape(8 * PART, 128).astype(f32),),
    )
    return (posteriors.T, log_norms[0])


def solution(mesh):
    split = Mesh(mesh.devices.reshape(8, 4, 4, 2, 2), SPLIT_AXES)
    return jax.shard_map(
        shards,
        mesh=split,
        in_specs=(
            P(SPLIT_AXES, None),
            P(SPLIT_AXES, None),
            P(SPLIT_AXES),
            P(),
            P(),
            P(),
            P(CLS, DOM),
        ),
        out_specs=(P(DOM, CLS), P(DOM)),
        check_vma=False,
    )
```

```python
import math

import jax
import jax.numpy as jnp
from jax import lax
from jax.experimental import pallas as pl
from jax.experimental.pallas import tpu as pltpu
from jax.sharding import Mesh
from jax.sharding import PartitionSpec as P

SIDE = 64
F = 2048
NT = 3
G = 16
PART = 128
JBLK = 72
SUB = 18
ROWS = 2 * JBLK
XF = F // 4
KX = 2 * XF + 128
SCALE = 32768.0
SPLIT_AXES = ("z", "yl", "x", "yh", "core")
DOM = ("z", "yl", "x")
CLS = ("yh", "core")
HIGH = lax.Precision.HIGHEST
NT_DIMS = (((1,), (1,)), ((), ()))


def phase_tables(offsets):
    freq_index = jnp.arange(F, dtype=jnp.int32)
    half_side = SIDE // 2
    row_freq = freq_index // half_side
    col_freq = freq_index % half_side
    row_freq = jnp.where(row_freq >= half_side, row_freq - SIDE, row_freq)
    turns = jnp.mod(offsets[:, 0:1] * row_freq[None, :] + offsets[:, 1:2] * col_freq[None, :], SIDE)
    angles = turns.astype(jnp.float32) * (2.0 * math.pi / SIDE)
    return (jnp.cos(angles), jnp.sin(angles))


def three_parts(value):
    first = value.astype(jnp.bfloat16).astype(jnp.float32)
    rest = value - first
    second = rest.astype(jnp.bfloat16).astype(jnp.float32)
    return (first, second, rest - second)


def turned(tiles, x):
    return jnp.concatenate([tile[:, x * 32 : x * 32 + 32] for tile in tiles], axis=1)


def shift_kernel(place_ref, images_ref, groups_ref, noise_ref, ctf_ref, cos_ref, sin_ref, out_ref):
    row = lax.broadcasted_iota(jnp.int32, (128, PART), 0)
    hot = jnp.where((row < 3 * G) & ((row & (G - 1)) == groups_ref[...]), 1.0, 0.0).T
    hot_parts = hot.astype(jnp.bfloat16)
    empty = jnp.zeros((128 - 3 * G, 128), jnp.bfloat16)
    own_terms = []
    for quad in range(4):
        real_tiles, imag_tiles = (tiles_of(images_ref, start) for start in (quad * 512, F + quad * 512))
        noise_tiles, ctf_tiles, cos_tiles, sin_tiles = (
            tiles_of(ref, quad * 512) for ref in (noise_ref, ctf_ref, cos_ref, sin_ref)
        )
        own = [turned(ref_tiles, 0) for ref_tiles in (noise_tiles, ctf_tiles)]
        for x in range(1, 4):
            here = place_ref[0] == x
            own[0] = jnp.where(here, turned(noise_tiles, x), own[0])
            own[1] = jnp.where(here, turned(ctf_tiles, x), own[1])
        own_terms.append(own[0] * own[1] * own[1])
        for x in range(4):
            real_part = turned(real_tiles, x)
            imag_part = turned(imag_tiles, x)
            noise = turned(noise_tiles, x)
            ctf = turned(ctf_tiles, x)
            cosines = turned(cos_tiles, x)
            sines = turned(sin_tiles, x)
            ctf_parts = jnp.concatenate(
                [part.astype(jnp.bfloat16) for part in three_parts(ctf)] + [empty], axis=0
            )
            weight = noise * jnp.dot(hot_parts, ctf_parts, preferred_element_type=jnp.float32)
            at = x * KX + quad * 128
            for t in range(NT):
                cosine = cosines[t : t + 1]
                sine = sines[t : t + 1]
                rows = slice(t * PART, (t + 1) * PART)
                out_ref[rows, at : at + 128] = (
                    weight * (real_part * cosine - imag_part * sine)
                ).astype(jnp.bfloat16)
                out_ref[rows, at + XF : at + XF + 128] = (
                    weight * (real_part * sine + imag_part * cosine)
                ).astype(jnp.bfloat16)
    minus = (-0.5 * hot).astype(jnp.bfloat16)
    for x in range(4):
        for t in range(NT):
            out_ref[t * PART : (t + 1) * PART, x * KX + 2 * XF : (x + 1) * KX] = minus
    for quad, term in enumerate(own_terms):
        for k, part in enumerate(three_parts(term)):
            for half in range(2):
                row, column = spare_place(quad * 2 + half)
                out_ref[row + k * G : row + (k + 1) * G, column : column + 64] = part[
                    :, half * 64 : half * 64 + 64
                ].astype(jnp.bfloat16)


def spare_place(n):
    return (n // 4 * 3 * G, n % 4 * KX + 2 * XF + 64)


def tiles_of(ref, start):
    return [
        ref[:, start + n * 128 : start + n * 128 + 128].astype(jnp.float32) for n in range(4)
    ]


def layout_kernel(plane_ref, shifted_ref, out_ref, rows_ref, small_ref, slabs_ref):
    for q in range(SUB // 2):
        pair = plane_ref[:, :, q * 128 : q * 128 + 128].astype(jnp.float32)
        slabs_ref[:, q : q + 1, :] = pair[:, 0:1]
        slabs_ref[:, q + SUB // 2 : q + SUB // 2 + 1, :] = pair[:, 1:2]
    for yh in range(2):
        for quad in range(8):
            tiles = [
                slabs_ref[(quad * 4 + n) * 2 + yh] for n in range(4)
            ]
            for s in range(4):
                at = (yh * 4 + s) * SUB
                rows_ref[at : at + SUB, quad * 128 : quad * 128 + 128] = turned(tiles, s)
    rows = rows_ref[...]
    out_ref[:, : 2 * XF] = rows.astype(jnp.bfloat16)
    square = rows * rows
    high = square.astype(jnp.bfloat16)
    low = (square - high.astype(jnp.float32)).astype(jnp.bfloat16)
    pieces = []
    for n in range(8):
        row, column = spare_place(n)
        pieces.append(shifted_ref[row : row + 3 * G, column : column + 64])
    parts = jnp.concatenate(pieces, axis=1)
    parts = jnp.concatenate([parts, parts], axis=1)
    sums = lax.dot_general(
        parts, high, NT_DIMS, preferred_element_type=jnp.float32
    ) + lax.dot_general(parts, low, NT_DIMS, preferred_element_type=jnp.float32)
    norms = sums[0:G] + (sums[G : 2 * G] + sums[2 * G : 3 * G])
    small_ref[...] = jnp.zeros_like(small_ref)
    for k, value in enumerate(three_parts(norms)):
        small_ref[k * G : (k + 1) * G, 0:ROWS] = value
    out_ref[:, 2 * XF :] = small_ref[...].T[0:ROWS].astype(jnp.bfloat16)


def product(shifted_ref, block_ref):
    total = None
    for x in range(4):
        part = lax.dot_general(
            shifted_ref[:, x * KX : (x + 1) * KX],
            block_ref[x],
            NT_DIMS,
            preferred_element_type=jnp.float32,
        )
        total = part if total is None else total + part
    return total


def half_kernel(place_ref, shifted_ref, mine_ref, target_ref, out_ref, chosen_ref, order_ref):
    out_ref[...] = product(shifted_ref, mine_ref)
    target = jnp.broadcast_to(target_ref[...].astype(jnp.float32), (PART, PART))
    row = lax.broadcasted_iota(jnp.int32, (PART, PART), 0)
    column = lax.broadcasted_iota(jnp.int32, (PART, PART), 1)
    earlier = jnp.where((target == target.T) & (row < column), 1.0, 0.0)
    slot_of = 2.0 * target[0:1] + jnp.sum(earlier, axis=0, keepdims=True)
    slot = lax.broadcasted_iota(jnp.int32, (2 * PART, PART), 0).astype(jnp.float32)
    chosen_ref[...] = jnp.where(slot == slot_of, 1.0, 0.0).astype(jnp.bfloat16)
    column = lax.broadcasted_iota(jnp.int32, (ROWS, 4 * 128), 1)
    lane = lax.broadcasted_iota(jnp.int32, (ROWS, 4 * 128), 0)
    block = column >> 7
    within = column & 127
    wanted = (block >> 1) * JBLK + (within & 3) * SUB + (within >> 2)
    kept = (within < JBLK) & (wanted == lane)
    for source in range(2):
        from_it = ((block & 1) ^ place_ref[1]) == source
        order_ref[source] = jnp.where(kept & from_it, 1.0, 0.0).astype(jnp.bfloat16)


def score_kernel(shifted_ref, other_ref, half_ref, chosen_ref, order_ref, out_ref, rest_ref):
    rest_ref[...] = product(shifted_ref, other_ref)
    scores = [
        [from_ref[t * PART : (t + 1) * PART, :] for t in range(NT)]
        for from_ref in (half_ref, rest_ref)
    ]
    tops = [jnp.maximum(jnp.maximum(s[0], s[1]), s[2]) for s in scores]
    peak = jnp.max(jnp.maximum(tops[0], tops[1]), axis=1, keepdims=True)
    raised = sum(jnp.exp(s - peak) for half in scores for s in half)
    log_norm = peak + jnp.log(jnp.sum(raised, axis=1, keepdims=True))
    column = lax.broadcasted_iota(jnp.int32, (PART, 4 * 128), 1)
    within = column & 127
    ordered = jnp.zeros((PART, 4 * 128), jnp.float32)
    for k, piece in enumerate(pieces_of(log_norm)):
        ordered = jnp.where(within == JBLK + k, piece, ordered)
    for source, half in enumerate(scores):
        posterior = SCALE * sum(jnp.exp(s - log_norm) for s in half)
        ordered += selected(posterior, order_ref[source])
    first, second, third = (
        jnp.dot(chosen_ref[...], part.astype(jnp.bfloat16), preferred_element_type=jnp.float32)
        for part in three_parts(ordered)
    )
    slots = first + (second + third)
    for block in range(4):
        out_ref[block * 2 * PART : (block + 1) * 2 * PART, :] = slots[
            :, block * 128 : (block + 1) * 128
        ]


def pieces_of(value):
    thousands = jnp.floor(value * (1.0 / 1024.0) + 0.5)
    rest = value - 1024.0 * thousands
    ones = jnp.floor(rest + 0.5)
    rest = (rest - ones) * 2048.0
    parts = jnp.floor(rest + 0.5)
    return (thousands, ones, parts, rest - parts)


def selected(values, one_hot):
    parts = jnp.concatenate([part.astype(jnp.bfloat16) for part in three_parts(values)], axis=0)
    each = jnp.dot(parts, one_hot, preferred_element_type=jnp.float32)
    count = values.shape[0]
    return each[0:count] + (each[count : 2 * count] + each[2 * count :])


def finish_kernel(slots_ref, posteriors_ref, log_norms_ref):
    rows = slots_ref[...].T
    posteriors_ref[...] = rows[0:JBLK] * (1.0 / SCALE)
    thousands, ones, parts, rest = (rows[JBLK + k : JBLK + k + 1] for k in range(4))
    log_norms_ref[...] = 1024.0 * thousands + (ones + (parts + rest) * (1.0 / 2048.0))


def call(kernel, name, outs, inputs, scratch=(), scalars=0):
    whole = pl.BlockSpec(memory_space=pltpu.VMEM)
    numbers = pl.BlockSpec(memory_space=pltpu.SMEM)
    shapes = [jax.ShapeDtypeStruct(shape, dtype) for shape, dtype in outs]
    results = pl.pallas_call(
        kernel,
        out_shape=shapes,
        in_specs=[numbers] * scalars + [whole] * (len(inputs) - scalars),
        out_specs=[whole] * len(outs),
        scratch_shapes=list(scratch),
        compiler_params=pltpu.CompilerParams(vmem_limit_bytes=24 * 1024 * 1024),
        name=name,
    )(*inputs)
    return results


def shards(images, destinations, group_ids, offsets, inv_noise, ctf_table, references):
    f32, bf16 = jnp.float32, jnp.bfloat16
    piece = references.reshape(2, SUB * 64)
    plane = lax.all_to_all(
        jnp.broadcast_to(piece[None], (64, 2, SUB * 64)), ("z", "yl", "yh"), 0, 0, tiled=True
    )
    place = jnp.stack([lax.axis_index("x"), lax.axis_index("core")]).astype(jnp.int32)
    cosines, sines = phase_tables(offsets)
    (shifted,) = call(
        shift_kernel,
        "shift",
        [((NT * PART, 4 * KX), bf16)],
        (place, images, group_ids[None, :], inv_noise[None, :], ctf_table, cosines, sines),
        scalars=1,
    )
    plane, shifted, place = lax.optimization_barrier((plane, shifted, place))
    (block,) = call(
        layout_kernel,
        "layout",
        [((ROWS, KX), bf16)],
        (plane, shifted),
        (
            pltpu.VMEM((ROWS, 2 * XF), f32),
            pltpu.VMEM((128, 256), f32),
            pltpu.VMEM((64, SUB, 128), f32),
        ),
    )
    mine = lax.all_to_all(jnp.broadcast_to(block[None], (4, ROWS, KX)), "x", 0, 0, tiled=True)
    other = lax.ppermute(mine, "core", [(0, 1), (1, 0)])
    half, chosen, order = call(
        half_kernel,
        "half",
        [((NT * PART, ROWS), f32), ((2 * PART, PART), bf16), ((2, ROWS, 4 * 128), bf16)],
        (place, shifted, mine, destinations.reshape(1, PART)),
        scalars=1,
    )
    (sends,) = call(
        score_kernel,
        "score",
        [((8 * PART, 128), f32)],
        (shifted, other, half, chosen, order),
        (pltpu.VMEM((NT * PART, ROWS), f32),),
    )
    sends = sends.astype(jnp.float16).reshape(4 * PART, 2, 128)
    whole = lax.all_to_all(sends, CLS + DOM, 0, 0, tiled=True)
    posteriors, log_norms = call(
        finish_kernel,
        "finish",
        [((JBLK, 8 * PART), f32), ((1, 8 * PART), f32)],
        (whole.reshape(8 * PART, 128).astype(f32),),
    )
    return (posteriors.T, log_norms[0])


def solution(mesh):
    split = Mesh(mesh.devices.reshape(8, 4, 4, 2, 2), SPLIT_AXES)
    return jax.shard_map(
        shards,
        mesh=split,
        in_specs=(
            P(SPLIT_AXES, None),
            P(SPLIT_AXES, None),
            P(SPLIT_AXES),
            P(),
            P(),
            P(),
            P(CLS, DOM),
        ),
        out_specs=(P(DOM, CLS), P(DOM)),
        check_vma=False,
    )
```

```python
import math

import jax
import jax.numpy as jnp
from jax import lax
from jax.experimental import pallas as pl
from jax.experimental.pallas import tpu as pltpu
from jax.sharding import Mesh
from jax.sharding import PartitionSpec as P

SIDE = 64
F = 2048
NT = 3
G = 16
PART = 128
JBLK = 72
SUB = 18
ROWS = 2 * JBLK
XF = F // 4
KX = 2 * XF + 128
SCALE = 32768.0
SPLIT_AXES = ("z", "yl", "x", "yh", "core")
DOM = ("z", "yl", "x")
CLS = ("yh", "core")
HIGH = lax.Precision.HIGHEST
NT_DIMS = (((1,), (1,)), ((), ()))


def phase_tables(offsets):
    freq_index = jnp.arange(F, dtype=jnp.int32)
    half_side = SIDE // 2
    row_freq = freq_index // half_side
    col_freq = freq_index % half_side
    row_freq = jnp.where(row_freq >= half_side, row_freq - SIDE, row_freq)
    turns = jnp.mod(offsets[:, 0:1] * row_freq[None, :] + offsets[:, 1:2] * col_freq[None, :], SIDE)
    angles = turns.astype(jnp.float32) * (2.0 * math.pi / SIDE)
    return (jnp.cos(angles), jnp.sin(angles))


def three_parts(value):
    first = value.astype(jnp.bfloat16).astype(jnp.float32)
    rest = value - first
    second = rest.astype(jnp.bfloat16).astype(jnp.float32)
    return (first, second, rest - second)


def turned(tiles, x):
    return jnp.concatenate([tile[:, x * 32 : x * 32 + 32] for tile in tiles], axis=1)


def shift_kernel(place_ref, images_ref, groups_ref, noise_ref, ctf_ref, cos_ref, sin_ref, out_ref):
    row = lax.broadcasted_iota(jnp.int32, (128, PART), 0)
    hot = jnp.where((row < 3 * G) & ((row & (G - 1)) == groups_ref[...]), 1.0, 0.0).T
    hot_parts = hot.astype(jnp.bfloat16)
    empty = jnp.zeros((128 - 3 * G, 128), jnp.bfloat16)
    own_terms = []
    for quad in range(4):
        real_tiles, imag_tiles = (tiles_of(images_ref, start) for start in (quad * 512, F + quad * 512))
        noise_tiles, ctf_tiles, cos_tiles, sin_tiles = (
            tiles_of(ref, quad * 512) for ref in (noise_ref, ctf_ref, cos_ref, sin_ref)
        )
        own = [turned(ref_tiles, 0) for ref_tiles in (noise_tiles, ctf_tiles)]
        for x in range(1, 4):
            here = place_ref[0] == x
            own[0] = jnp.where(here, turned(noise_tiles, x), own[0])
            own[1] = jnp.where(here, turned(ctf_tiles, x), own[1])
        own_terms.append(own[0] * own[1] * own[1])
        for x in range(4):
            real_part = turned(real_tiles, x)
            imag_part = turned(imag_tiles, x)
            noise = turned(noise_tiles, x)
            ctf = turned(ctf_tiles, x)
            cosines = turned(cos_tiles, x)
            sines = turned(sin_tiles, x)
            ctf_parts = jnp.concatenate(
                [part.astype(jnp.bfloat16) for part in three_parts(ctf)] + [empty], axis=0
            )
            weight = noise * jnp.dot(hot_parts, ctf_parts, preferred_element_type=jnp.float32)
            at = x * KX + quad * 128
            for t in range(NT):
                cosine = cosines[t : t + 1]
                sine = sines[t : t + 1]
                rows = slice(t * PART, (t + 1) * PART)
                out_ref[rows, at : at + 128] = (
                    weight * (real_part * cosine - imag_part * sine)
                ).astype(jnp.bfloat16)
                out_ref[rows, at + XF : at + XF + 128] = (
                    weight * (real_part * sine + imag_part * cosine)
                ).astype(jnp.bfloat16)
    minus = (-0.5 * hot).astype(jnp.bfloat16)
    for x in range(4):
        for t in range(NT):
            out_ref[t * PART : (t + 1) * PART, x * KX + 2 * XF : (x + 1) * KX] = minus
    for quad, term in enumerate(own_terms):
        for k, part in enumerate(three_parts(term)):
            for half in range(2):
                row, column = spare_place(quad * 2 + half)
                out_ref[row + k * G : row + (k + 1) * G, column : column + 64] = part[
                    :, half * 64 : half * 64 + 64
                ].astype(jnp.bfloat16)


def spare_place(n):
    return (n // 4 * 3 * G, n % 4 * KX + 2 * XF + 64)


def tiles_of(ref, start):
    return [
        ref[:, start + n * 128 : start + n * 128 + 128].astype(jnp.float32) for n in range(4)
    ]


def layout_kernel(plane_ref, shifted_ref, out_ref, rows_ref, small_ref, slabs_ref):
    for q in range(SUB // 2):
        pair = plane_ref[:, :, q * 128 : q * 128 + 128].astype(jnp.float32)
        slabs_ref[:, q : q + 1, :] = pair[:, 0:1]
        slabs_ref[:, q + SUB // 2 : q + SUB // 2 + 1, :] = pair[:, 1:2]
    for yh in range(2):
        for quad in range(8):
            tiles = [
                slabs_ref[(quad * 4 + n) * 2 + yh] for n in range(4)
            ]
            for s in range(4):
                at = (yh * 4 + s) * SUB
                rows_ref[at : at + SUB, quad * 128 : quad * 128 + 128] = turned(tiles, s)
    rows = rows_ref[...]
    out_ref[:, : 2 * XF] = rows.astype(jnp.bfloat16)
    square = rows * rows
    high = square.astype(jnp.bfloat16)
    low = (square - high.astype(jnp.float32)).astype(jnp.bfloat16)
    pieces = []
    for n in range(8):
        row, column = spare_place(n)
        pieces.append(shifted_ref[row : row + 3 * G, column : column + 64])
    parts = jnp.concatenate(pieces, axis=1)
    parts = jnp.concatenate([parts, parts], axis=1)
    sums = lax.dot_general(
        parts, high, NT_DIMS, preferred_element_type=jnp.float32
    ) + lax.dot_general(parts, low, NT_DIMS, preferred_element_type=jnp.float32)
    norms = sums[0:G] + (sums[G : 2 * G] + sums[2 * G : 3 * G])
    small_ref[...] = jnp.zeros_like(small_ref)
    for k, value in enumerate(three_parts(norms)):
        small_ref[k * G : (k + 1) * G, 0:ROWS] = value
    out_ref[:, 2 * XF :] = small_ref[...].T[0:ROWS].astype(jnp.bfloat16)


def product(shifted_ref, block_ref):
    total = None
    for x in range(4):
        part = lax.dot_general(
            shifted_ref[:, x * KX : (x + 1) * KX],
            block_ref[x],
            NT_DIMS,
            preferred_element_type=jnp.float32,
        )
        total = part if total is None else total + part
    return total


def half_kernel(place_ref, shifted_ref, mine_ref, target_ref, out_ref, chosen_ref, order_ref):
    out_ref[...] = product(shifted_ref, mine_ref)
    target = jnp.broadcast_to(target_ref[...].astype(jnp.float32), (PART, PART))
    row = lax.broadcasted_iota(jnp.int32, (PART, PART), 0)
    column = lax.broadcasted_iota(jnp.int32, (PART, PART), 1)
    earlier = jnp.where((target == target.T) & (row < column), 1.0, 0.0)
    slot_of = 2.0 * target[0:1] + jnp.sum(earlier, axis=0, keepdims=True)
    slot = lax.broadcasted_iota(jnp.int32, (2 * PART, PART), 0).astype(jnp.float32)
    chosen_ref[...] = jnp.where(slot == slot_of, 1.0, 0.0).astype(jnp.bfloat16)
    column = lax.broadcasted_iota(jnp.int32, (ROWS, 4 * 128), 1)
    lane = lax.broadcasted_iota(jnp.int32, (ROWS, 4 * 128), 0)
    block = column >> 7
    within = column & 127
    wanted = (block >> 1) * JBLK + (within & 3) * SUB + (within >> 2)
    kept = (within < JBLK) & (wanted == lane)
    for source in range(2):
        from_it = ((block & 1) ^ place_ref[1]) == source
        order_ref[source] = jnp.where(kept & from_it, 1.0, 0.0).astype(jnp.bfloat16)


def score_kernel(shifted_ref, other_ref, half_ref, chosen_ref, order_ref, out_ref, rest_ref):
    rest_ref[...] = product(shifted_ref, other_ref)
    scores = [
        [from_ref[t * PART : (t + 1) * PART, :] for t in range(NT)]
        for from_ref in (half_ref, rest_ref)
    ]
    tops = [jnp.maximum(jnp.maximum(s[0], s[1]), s[2]) for s in scores]
    peak = jnp.max(jnp.maximum(tops[0], tops[1]), axis=1, keepdims=True)
    raised = [sum(jnp.exp(s - peak) for s in half) for half in scores]
    log_norm = peak + jnp.log(jnp.sum(raised[0] + raised[1], axis=1, keepdims=True))
    shrink = SCALE * jnp.exp(peak - log_norm)
    column = lax.broadcasted_iota(jnp.int32, (PART, 4 * 128), 1)
    within = column & 127
    ordered = jnp.zeros((PART, 4 * 128), jnp.float32)
    for k, piece in enumerate(pieces_of(log_norm)):
        ordered = jnp.where(within == JBLK + k, piece, ordered)
    for source, half in enumerate(raised):
        posterior = shrink * half
        ordered += selected(posterior, order_ref[source])
    first, second, third = (
        jnp.dot(chosen_ref[...], part.astype(jnp.bfloat16), preferred_element_type=jnp.float32)
        for part in three_parts(ordered)
    )
    slots = first + (second + third)
    for block in range(4):
        out_ref[block * 2 * PART : (block + 1) * 2 * PART, :] = slots[
            :, block * 128 : (block + 1) * 128
        ]


def pieces_of(value):
    thousands = jnp.floor(value * (1.0 / 1024.0) + 0.5)
    rest = value - 1024.0 * thousands
    ones = jnp.floor(rest + 0.5)
    rest = (rest - ones) * 2048.0
    parts = jnp.floor(rest + 0.5)
    return (thousands, ones, parts, rest - parts)


def selected(values, one_hot):
    parts = jnp.concatenate([part.astype(jnp.bfloat16) for part in three_parts(values)], axis=0)
    each = jnp.dot(parts, one_hot, preferred_element_type=jnp.float32)
    count = values.shape[0]
    return each[0:count] + (each[count : 2 * count] + each[2 * count :])


def finish_kernel(slots_ref, posteriors_ref, log_norms_ref):
    rows = slots_ref[...].T
    posteriors_ref[...] = rows[0:JBLK] * (1.0 / SCALE)
    thousands, ones, parts, rest = (rows[JBLK + k : JBLK + k + 1] for k in range(4))
    log_norms_ref[...] = 1024.0 * thousands + (ones + (parts + rest) * (1.0 / 2048.0))


def call(kernel, name, outs, inputs, scratch=(), scalars=0):
    whole = pl.BlockSpec(memory_space=pltpu.VMEM)
    numbers = pl.BlockSpec(memory_space=pltpu.SMEM)
    shapes = [jax.ShapeDtypeStruct(shape, dtype) for shape, dtype in outs]
    results = pl.pallas_call(
        kernel,
        out_shape=shapes,
        in_specs=[numbers] * scalars + [whole] * (len(inputs) - scalars),
        out_specs=[whole] * len(outs),
        scratch_shapes=list(scratch),
        compiler_params=pltpu.CompilerParams(vmem_limit_bytes=24 * 1024 * 1024),
        name=name,
    )(*inputs)
    return results


def shards(images, destinations, group_ids, offsets, inv_noise, ctf_table, references):
    f32, bf16 = jnp.float32, jnp.bfloat16
    piece = references.reshape(2, SUB * 64)
    plane = lax.all_to_all(
        jnp.broadcast_to(piece[None], (64, 2, SUB * 64)), ("z", "yl", "yh"), 0, 0, tiled=True
    )
    place = jnp.stack([lax.axis_index("x"), lax.axis_index("core")]).astype(jnp.int32)
    cosines, sines = phase_tables(offsets)
    (shifted,) = call(
        shift_kernel,
        "shift",
        [((NT * PART, 4 * KX), bf16)],
        (place, images, group_ids[None, :], inv_noise[None, :], ctf_table, cosines, sines),
        scalars=1,
    )
    plane, shifted, place = lax.optimization_barrier((plane, shifted, place))
    (block,) = call(
        layout_kernel,
        "layout",
        [((ROWS, KX), bf16)],
        (plane, shifted),
        (
            pltpu.VMEM((ROWS, 2 * XF), f32),
            pltpu.VMEM((128, 256), f32),
            pltpu.VMEM((64, SUB, 128), f32),
        ),
    )
    mine = lax.all_to_all(jnp.broadcast_to(block[None], (4, ROWS, KX)), "x", 0, 0, tiled=True)
    other = lax.ppermute(mine, "core", [(0, 1), (1, 0)])
    half, chosen, order = call(
        half_kernel,
        "half",
        [((NT * PART, ROWS), f32), ((2 * PART, PART), bf16), ((2, ROWS, 4 * 128), bf16)],
        (place, shifted, mine, destinations.reshape(1, PART)),
        scalars=1,
    )
    (sends,) = call(
        score_kernel,
        "score",
        [((8 * PART, 128), f32)],
        (shifted, other, half, chosen, order),
        (pltpu.VMEM((NT * PART, ROWS), f32),),
    )
    sends = sends.astype(jnp.float16).reshape(4 * PART, 2, 128)
    whole = lax.all_to_all(sends, CLS + DOM, 0, 0, tiled=True)
    posteriors, log_norms = call(
        finish_kernel,
        "finish",
        [((JBLK, 8 * PART), f32), ((1, 8 * PART), f32)],
        (whole.reshape(8 * PART, 128).astype(f32),),
    )
    return (posteriors.T, log_norms[0])


def solution(mesh):
    split = Mesh(mesh.devices.reshape(8, 4, 4, 2, 2), SPLIT_AXES)
    return jax.shard_map(
        shards,
        mesh=split,
        in_specs=(
            P(SPLIT_AXES, None),
            P(SPLIT_AXES, None),
            P(SPLIT_AXES),
            P(),
            P(),
            P(),
            P(CLS, DOM),
        ),
        out_specs=(P(DOM, CLS), P(DOM)),
        check_vma=False,
    )
```
